128 devices in a mesh: row: 8 (over x_hi, z), col: 16 (over x_lo, y, core).
Axes of the slice: x: 4 (x_hi: 2, x_lo: 2; x = x_hi * 2 + x_lo), y: 4, z: 4, core: 2. Of those that a mesh axis runs over, the one named last changes fastest.
Arguments:
- tangents: float32 [3, 512, 512, 128], P(None, 'row', 'col'), may hold values from -400 to 400
- sea_mask: int32 [512, 512], P('row', 'col'), may hold values 0 or 1
- levels: int32 [512, 512], P('row', 'col'), may hold values from 0 to 49
- current: float32 [512, 512], P('row', 'col'), may hold values from -0.6 to 0.6
Outputs:
- new_tangents: float32 [3, 512, 512, 128], P(None, 'row', 'col')
- growth: float32 [128], replicated
The draws below stay inside these ranges and needn't reach their ends.
All inputs are finite; a program needn't handle non-finite values. No bound on the sum of `sea_mask` on one device may be relied on, other than what follows from the above.
Results may differ from the reference program's by a relative error of at most 0.00014.
Values sent between devices are 32-bit elements; how exact they have to be, the bound alone decides.
A program may use at most 64 MiB of HBM per device.

```python
import math
import jax
import jax.numpy as jnp
from jax import lax

MODES = 128
STEPS = 2
RENORMS = 2
LEVELS = 50
NLAT = 512
NLON = 512


def draw_tangents(key, part):
    base_key = jax.random.fold_in(key, 11)
    key_noise, key_cell, key_mode = jax.random.split(base_key, 3)
    latitude = jnp.arange(NLAT, dtype=jnp.float32)[:, None] / NLAT
    longitude = jnp.arange(NLON, dtype=jnp.float32)[None, :] / NLON
    cell_scale = jnp.exp(jax.random.uniform(key_cell, (NLAT, NLON)) * math.log(10.0))
    mode_scale = jnp.exp(jax.random.uniform(key_mode, (MODES,)) * math.log(10.0))
    trend_scale = jnp.exp((latitude + longitude) * math.log(3.0))
    random_part = jnp.clip(jax.random.normal(key_noise, (3, NLAT, NLON, MODES)), -4.0, 4.0)
    return (0.1 * random_part * (cell_scale * trend_scale)[None, :, :, None] * mode_scale).astype(jnp.float32)


def set_ends(array, key, low, top_value):
    longest = array.shape.index(max(array.shape))
    spots = []
    for shift in (0, 1):
        where = [jax.random.randint(jax.random.fold_in(key, axis), (), 0, length) for axis, length in enumerate(array.shape)]
        where[longest] = (where[longest] + shift) % array.shape[longest]
        spots.append(tuple(where))
    return array.at[spots[0]].set(low).at[spots[1]].set(top_value)


def steps_of(rng, shape, shards, low, largest):
    loudness, own = 1.0, jax.random.fold_in(rng, 6)
    for dim, shards_of in shards:
        steps = jnp.exp(jax.random.uniform(jax.random.fold_in(own, dim), (shards_of,), jnp.float32, low / len(shards), largest / len(shards)))
        loudness = loudness * jnp.repeat(steps, shape[dim] // shards_of).reshape([-1 if axis == dim else 1 for axis in range(len(shape))])
    return loudness


def setup_inputs(seed: int = 0) -> dict:
    streams_of = jax.random.split(jax.random.key(seed), 5)
    return {
        "tangents": draw_tangents(jax.random.fold_in(streams_of[4], 71), 0),
        "sea_mask": set_ends((jax.random.randint(streams_of[1], (NLAT, NLON), 0, 5) < 4).astype(jnp.int32), jax.random.fold_in(streams_of[1], 1), 0, 1),
        "levels": set_ends(jax.random.randint(streams_of[2], (NLAT, NLON), 0, LEVELS), jax.random.fold_in(streams_of[2], 1), 0, LEVELS - 1).astype(jnp.int32),
        "current": jnp.clip(jax.random.uniform(streams_of[3], (NLAT, NLON), jnp.float32, -0.6, 0.6) * steps_of(streams_of[3], (NLAT, NLON), ((0, 8), (1, 16)), -0.4, 0.0), -0.6, 0.6),
    }


viscosity = 0.15
gravity = 0.5
rotation = 0.4

def latitude_spin(rows_global, total_rows):
    angle = (-70.0 + 140.0 * (rows_global + 0.5) / total_rows) * (jnp.pi / 180.0)
    return rotation * jnp.sin(angle)

def advance(padded, sea_frac, column_depth, current, coriolis):
    middle = padded[:, 1:-1, 1:-1]
    east_side = padded[:, 1:-1, 2:]
    west_side = padded[:, 1:-1, :-2]
    north_side = padded[:, 2:, 1:-1]
    south_side = padded[:, :-2, 1:-1]
    zonal_diff = 0.5 * (east_side - west_side)
    merid_diff = 0.5 * (north_side - south_side)
    spread = east_side + west_side + north_side + south_side - 4.0 * middle
    advected = middle + viscosity * spread - current * zonal_diff
    zonal = sea_frac * (advected[0] - gravity * zonal_diff[2] + coriolis * middle[1])
    meridional = sea_frac * (advected[1] - gravity * merid_diff[2] - coriolis * middle[0])
    height = sea_frac * (advected[2] - column_depth * (zonal_diff[0] + merid_diff[1]))
    return jnp.stack([zonal, meridional, height])

def pad_global(field):
    rowed = jnp.pad(field, ((0, 0), (1, 1), (0, 0), (0, 0)))
    return jnp.concatenate([rowed[:, :, -1:], rowed, rowed[:, :, :1]], axis=2)

def reference(tangents, sea_mask, levels, current):
    sea_frac = sea_mask.astype(jnp.float32)[:, :, None]
    column_depth = ((levels + 1).astype(jnp.float32) / LEVELS)[:, :, None]
    flow = current[:, :, None]
    coriolis = latitude_spin(jnp.arange(NLAT, dtype=jnp.float32), NLAT)[:, None, None]
    group_width = MODES // 8
    growth = jnp.zeros((MODES,), jnp.float32)
    identity = jnp.eye(MODES, dtype=jnp.float32)
    for renorm in range(RENORMS):
        pieces = []
        for group in range(8):
            piece = tangents[:, :, :, group * group_width:(group + 1) * group_width]
            for substep in range(STEPS):
                piece = advance(pad_global(piece), sea_frac, column_depth, flow, coriolis)
            pieces.append(piece)
        tangents = jnp.concatenate(pieces, axis=3)
        flattened = tangents.reshape(-1, MODES)
        gram_matrix = lax.dot_general(flattened, flattened, (((0,), (0,)), ((), ())), precision=lax.Precision.HIGHEST) / (NLAT * NLON)
        lower_factor = jnp.linalg.cholesky(gram_matrix)
        inverse_factor = jax.scipy.linalg.solve_triangular(lower_factor, identity, lower=True)
        tangents = jnp.dot(flattened, inverse_factor.T, precision=lax.Precision.HIGHEST).reshape(tangents.shape)
        growth = growth + jnp.log(jnp.diagonal(lower_factor))
    return (tangents, growth)
```

```python
import jax
import jax.numpy as jnp
from jax import lax
from jax.experimental import pallas as pl
from jax.experimental.pallas import tpu as pltpu
from jax.sharding import PartitionSpec as P

MESH = pl.DeviceIdType.MESH
F32 = jnp.float32
BF16 = jnp.bfloat16
ROWS, COLS = 8, 16
LAT, LON, MODES = 64, 32, 128
LEVELS = 50
CELLS = 512 * 512
ANY = pl.BlockSpec(memory_space=pl.ANY)
VMEM = pl.BlockSpec(memory_space=pltpu.VMEM)


def vmem(*shape):
    return pltpu.VMEM(shape, F32)


def remote(src, dst, sems, k, dev):
    return pltpu.make_async_remote_copy(
        src_ref=src, dst_ref=dst, send_sem=sems.at[2 * k], recv_sem=sems.at[2 * k + 1], device_id=dev, device_id_type=MESH
    )


def at(row, col):
    return {"row": row, "col": col}


def shift(row, col, drow, dcol):
    return at(lax.rem(row + drow + ROWS, ROWS), lax.rem(col + dcol + COLS, COLS))


def inner_peer(row, col, d):
    member = lax.rem(lax.rem(col, 8) + d, 8)
    return member, at(row, (col // 8) * 8 + member)


def outer_index(row, col):
    return (col // 8) * 8 + row


def outer_peer(row, col, d):
    k = lax.rem(outer_index(row, col) + d, 16)
    return at(lax.rem(k, 8), (k // 8) * 8 + lax.rem(col, 8))


NEIGHBOURS = [(0, -1), (0, 1), (-1, 0), (1, 0), (-1, -1), (-1, 1), (1, -1), (1, 1)]


def greet(row, col, halo):
    barrier = pltpu.get_barrier_semaphore()
    peers = [inner_peer(row, col, d)[1] for d in range(1, 8)] + [outer_peer(row, col, d) for d in range(1, 16)]
    if halo:
        peers += [shift(row, col, a, b) for a, b in NEIGHBOURS]
    for dev in peers:
        pl.semaphore_signal(barrier, inc=1, device_id=dev, device_id_type=MESH)
    return lambda: pl.semaphore_wait(barrier, len(peers))


class Reduce:
    def __init__(self, row, col, g, inner, part, outer, total, sems):
        self.row, self.col = row, col
        self.g, self.inner, self.part, self.outer, self.total, self.sems = g, inner, part, outer, total, sems
        self.me = lax.rem(col, 8)
        self.waits = []

    def scatter(self):
        for d in range(1, 8):
            member, dev = inner_peer(self.row, self.col, d)
            remote(self.g.at[member], self.inner.at[d], self.sems, 0, dev).start()

    def exchange(self):
        w = remote(self.inner.at[pl.ds(1, 7)], self.inner.at[pl.ds(1, 7)], self.sems, 0, inner_peer(self.row, self.col, 1)[1])
        w.wait_recv()
        s = self.g[self.me]
        for d in range(1, 8):
            s = s + self.inner[d]
        self.part[...] = s
        k = outer_index(self.row, self.col)
        for d in range(1, 16):
            remote(self.part, self.outer.at[k], self.sems, 1, outer_peer(self.row, self.col, d)).start()
        self.outer[k] = s
        self.waits.append(w)

    def gather(self):
        w = remote(self.outer.at[pl.ds(0, 15)], self.outer.at[pl.ds(0, 15)], self.sems, 1, outer_peer(self.row, self.col, 1))
        w.wait_recv()
        t = self.outer[0]
        for e in range(1, 16):
            t = t + self.outer[e]
        self.total[self.me] = t
        for d in range(1, 8):
            remote(self.total.at[self.me], self.total.at[self.me], self.sems, 2, inner_peer(self.row, self.col, d)[1]).start()
        self.waits.append(w)

    def finish(self):
        w = remote(self.total.at[pl.ds(0, 7)], self.total.at[pl.ds(0, 7)], self.sems, 2, inner_peer(self.row, self.col, 1)[1])
        w.wait_recv()
        self.waits.append(w)
        for w in self.waits:
            w.wait_send()
        return self.total[...].reshape(MODES, MODES)


REDUCE_SCRATCH = [vmem(8, 16, 128), vmem(8, 16, 128), vmem(16, 128), vmem(16, 16, 128), vmem(8, 16, 128)]


def split(x):
    hi = x.astype(BF16)
    return hi, (x - hi.astype(F32)).astype(BF16)


def gram_of(x):
    hi, lo = split(x)
    return lax.dot_general(hi, jnp.concatenate([hi, lo], axis=1), (((0,), (0,)), ((), ())), preferred_element_type=F32)


def close_gram(acc):
    cross = acc[:, 128:]
    return (acc[:, :128] + cross + cross.T) * (1.0 / CELLS)


def weights_of(inverse):
    hi, lo = split(inverse)
    return jnp.concatenate(
        [jnp.concatenate([hi, hi], axis=1), jnp.concatenate([lo, jnp.zeros_like(lo)], axis=1)], axis=0
    )


def apply_inverse(x, weights):
    hi, lo = split(x)
    both = lax.dot_general(
        jnp.concatenate([hi, lo], axis=1), weights, (((1,), (1,)), ((), ())), preferred_element_type=F32
    )
    return both[:, :128] + both[:, 128:]


def model_step(src, src_row, dst, dst_row, planes, spin, plane_row, rows, starts):
    @pl.loop(0, rows)
    def _(i):
        r, p, o = src_row + i, plane_row + i, dst_row + i
        cor = jnp.broadcast_to(spin[pl.ds(p, 1), :], (8, 128))
        for s in starts:
            here = pl.ds(s, 8)
            sea, flow, deep = planes[0, p, here, :], planes[1, p, here, :], planes[2, p, here, :]
            mid = [src[q, r, here, :] for q in range(3)]
            east = [src[q, r, pl.ds(s + 1, 8), :] for q in range(3)]
            west = [src[q, r, pl.ds(s - 1, 8), :] for q in range(3)]
            north = [src[q, r + 1, here, :] for q in range(3)]
            south = [src[q, r - 1, here, :] for q in range(3)]
            along = [east[q] - west[q] for q in range(3)]
            moved = [
                0.4 * mid[q] + 0.15 * ((east[q] + west[q]) + (north[q] + south[q])) - flow * along[q] for q in range(3)
            ]
            dst[0, o, here, :] = sea * (moved[0] - 0.25 * along[2] + cor * mid[1])
            dst[1, o, here, :] = sea * (moved[1] - 0.25 * (north[2] - south[2]) - cor * mid[0])
            dst[2, o, here, :] = sea * (moved[2] - deep * (along[0] + (north[1] - south[1])))


OUTER_STARTS = (7, 15, 23, 31, 39)
INNER_STARTS = (8, 16, 24, 32)


def start_kernel(
    x_hbm, mask_ref, levels_ref, current_ref, c_hbm, gram_ref,
    x, y, planes, table, north_table, south_table, spin, acc,
    send_w, send_e, recv_w, recv_e, send_k, recv_k, ghost,
    g, inner, part, outer, total, sems, hsems, lsem,
):
    row, col = lax.axis_index("row"), lax.axis_index("col")
    load = pltpu.make_async_copy(x_hbm, x.at[:, pl.ds(2, LAT), pl.ds(8, LON), :], lsem.at[0])
    load.start()
    wait_barrier = greet(row, col, True)

    packed = jnp.concatenate(
        [
            mask_ref[...].astype(F32),
            0.5 * current_ref[...],
            0.5 * ((levels_ref[...] + 1).astype(F32) / LEVELS),
            jnp.zeros((LAT, 32), F32),
        ],
        axis=1,
    )
    turned = jnp.concatenate([packed, jnp.zeros((64, 128), F32)], axis=0).T
    for k in range(3):
        table[k, 8:40, :] = turned[32 * k : 32 * k + 32, :]
    lat = lax.broadcasted_iota(jnp.int32, (72, 128), 0) + row * LAT - 1
    angle = (-70.0 + 140.0 * (lat.astype(F32) + 0.5) / (ROWS * LAT)) * (jnp.pi / 180.0)
    spin[...] = 0.4 * jnp.sin(angle)

    def row_copies(e, src, off, k):
        width = slice(None) if off == 0 else pl.ds(8, LON)
        return [
            remote(src.at[:, pl.ds(off, 2), width, :], ghost.at[e, 1], hsems, k, shift(row, col, -1, 0)),
            remote(src.at[:, pl.ds(off + 62, 2), width, :], ghost.at[e, 0], hsems, k + 1, shift(row, col, 1, 0)),
        ]

    def pack():
        @pl.loop(0, 16)
        def _(j):
            for q in range(3):
                for m in range(4):
                    send_w[q, j, 2 * m : 2 * m + 2, :] = x[q, 4 * j + m + 2, 8:10, :]
                    send_e[q, j, 2 * m : 2 * m + 2, :] = x[q, 4 * j + m + 2, 38:40, :]

        for c, (i, j) in enumerate(((2, 8), (2, 39), (65, 8), (65, 39))):
            for q in range(3):
                send_k[c, q : q + 1, :] = x[q, i, j : j + 1, :]

    def side_copies(e, k):
        out = [
            remote(send_w, recv_e.at[e], hsems, k, shift(row, col, 0, -1)),
            remote(send_e, recv_w.at[e], hsems, k + 1, shift(row, col, 0, 1)),
        ]
        for c, (a, b) in enumerate(((-1, -1), (-1, 1), (1, -1), (1, 1))):
            out.append(remote(send_k.at[c], recv_k.at[e, 3 - c], hsems, k + 2 + c, shift(row, col, a, b)))
        return out

    def unpack(e):
        @pl.loop(0, 16)
        def _(j):
            for q in range(3):
                for m in range(4):
                    x[q, 4 * j + m + 2, 6:8, :] = recv_w[e, q, j, 2 * m : 2 * m + 2, :]
                    x[q, 4 * j + m + 2, 40:42, :] = recv_e[e, q, j, 2 * m : 2 * m + 2, :]

        for c, (i, j) in enumerate(((1, 7), (1, 40), (66, 7), (66, 40))):
            for q in range(3):
                x[q, i, j : j + 1, :] = recv_k[e, c, q : q + 1, :]

        x[:, 0:2, 8:40, :] = ghost[e, 0]
        x[:, 66:68, 8:40, :] = ghost[e, 1]

        @pl.when(row == 0)
        def _():
            x[:, 0:2, :, :] = jnp.zeros((3, 2, 48, 128), F32)

        @pl.when(row == ROWS - 1)
        def _():
            x[:, 66:68, :, :] = jnp.zeros((3, 2, 48, 128), F32)

    wait_barrier()
    tables = [
        remote(table.at[:, pl.ds(8, 8), :], table.at[:, pl.ds(40, 8), :], hsems, 8, shift(row, col, 0, -1)),
        remote(table.at[:, pl.ds(32, 8), :], table.at[:, pl.ds(0, 8), :], hsems, 9, shift(row, col, 0, 1)),
        remote(table.at[:, pl.ds(8, 32), :], north_table, hsems, 10, shift(row, col, -1, 0)),
        remote(table.at[:, pl.ds(8, 32), :], south_table, hsems, 11, shift(row, col, 1, 0)),
    ]
    first = row_copies(0, x_hbm, 0, 0)
    for copy in tables + first:
        copy.start()
    load.wait()
    pack()
    sides = side_copies(0, 2)
    for copy in sides:
        copy.start()

    def spread(k, tile):
        start = pl.multiple_of(8 * tile, 8)
        lanes = table[k, pl.ds(start, 8), :]
        for i in range(LAT):
            planes[k, i + 1, pl.ds(start, 8), :] = jnp.broadcast_to(lanes[:, i : i + 1], (8, 128))

    for k in range(3):
        @pl.loop(1, 5)
        def _(tile):
            spread(k, tile)

    for copy in tables:
        copy.wait()
    for k in range(3):
        @pl.loop(0, 2)
        def _(edge):
            spread(k, 5 * edge)

        for tile in range(4):
            planes[k, 65, 8 * tile + 8 : 8 * tile + 16, :] = jnp.broadcast_to(north_table[k, 8 * tile : 8 * tile + 8, 0:1], (8, 128))
            planes[k, 0, 8 * tile + 8 : 8 * tile + 16, :] = jnp.broadcast_to(south_table[k, 8 * tile : 8 * tile + 8, 63:64], (8, 128))

    @pl.when(row == 0)
    def _():
        planes[0, 0, :, :] = jnp.zeros((48, 128), F32)

    @pl.when(row == ROWS - 1)
    def _():
        planes[0, 65, :, :] = jnp.zeros((48, 128), F32)

    for copy in first + sides:
        copy.wait()
    unpack(0)
    model_step(x, 1, y, 0, planes, spin, 0, LAT + 2, OUTER_STARTS)
    model_step(y, 1, x, 2, planes, spin, 1, LAT, INNER_STARTS)

    acc[...] = jnp.zeros_like(acc)

    @pl.loop(0, 8)
    def _(j):
        for q in range(3):
            acc[...] += gram_of(x[q, pl.ds(8 * j + 2, 8), 8:40, :].reshape(256, 128))

    g[...] = close_gram(acc[...]).reshape(8, 16, 128)
    reduce = Reduce(row, col, g, inner, part, outer, total, sems)
    reduce.scatter()
    pack()
    halo = row_copies(1, x, 2, 12) + side_copies(1, 14)
    for copy in halo:
        copy.start()
    reduce.exchange()
    for copy in halo:
        copy.wait()
    unpack(1)
    model_step(x, 1, y, 0, planes, spin, 0, LAT + 2, OUTER_STARTS)
    reduce.gather()
    model_step(y, 1, x, 2, planes, spin, 1, LAT, INNER_STARTS)
    store = pltpu.make_async_copy(x.at[:, pl.ds(2, LAT), pl.ds(8, LON), :], c_hbm, lsem.at[0])
    store.start()
    gram_ref[...] = reduce.finish()
    store.wait()


def start(tangents, sea_mask, levels, current):
    return pl.pallas_call(
        start_kernel,
        out_shape=(jax.ShapeDtypeStruct(tangents.shape, F32), jax.ShapeDtypeStruct((MODES, MODES), F32)),
        in_specs=[ANY, VMEM, VMEM, VMEM],
        out_specs=(ANY, VMEM),
        scratch_shapes=[
            vmem(3, 68, 48, 128), vmem(3, 66, 48, 128), vmem(3, 66, 48, 128), vmem(3, 48, 128), vmem(3, 32, 128),
            vmem(3, 32, 128), vmem(72, 128), vmem(128, 256),
            vmem(3, 16, 8, 128), vmem(3, 16, 8, 128), vmem(2, 3, 16, 8, 128), vmem(2, 3, 16, 8, 128), vmem(4, 8, 128), vmem(2, 4, 8, 128),
            vmem(2, 2, 3, 2, LON, 128),
            *REDUCE_SCRATCH,
            pltpu.SemaphoreType.DMA((6,)), pltpu.SemaphoreType.DMA((40,)), pltpu.SemaphoreType.DMA((1,)),
        ],
        compiler_params=pltpu.CompilerParams(collective_id=0, has_side_effects=True, vmem_limit_bytes=48 * 2**20),
        name="start",
    )(tangents, sea_mask, levels, current)


def normalise_kernel(c_hbm, inverse_ref, b_hbm, gram_ref, x, acc, g, inner, part, outer, total, sems, lsem):
    row, col = lax.axis_index("row"), lax.axis_index("col")
    pieces = 8
    loads = [pltpu.make_async_copy(c_hbm.at[pl.ds(768 * k, 768)], x.at[pl.ds(768 * k, 768)], lsem.at[k]) for k in range(pieces)]
    stores = [pltpu.make_async_copy(x.at[pl.ds(768 * k, 768)], b_hbm.at[pl.ds(768 * k, 768)], lsem.at[k]) for k in range(pieces)]
    for copy in loads:
        copy.start()
    wait_barrier = greet(row, col, False)
    weights = weights_of(inverse_ref[...])
    acc[...] = jnp.zeros_like(acc)
    for k in range(pieces):
        loads[k].wait()

        @pl.loop(0, 3)
        def _(j):
            here = pl.ds(pl.multiple_of(768 * k + 256 * j, 256), 256)
            b = apply_inverse(x[here, :], weights)
            x[here, :] = b
            acc[...] += gram_of(b)

        stores[k].start()
    g[...] = close_gram(acc[...]).reshape(8, 16, 128)
    wait_barrier()
    reduce = Reduce(row, col, g, inner, part, outer, total, sems)
    reduce.scatter()
    reduce.exchange()
    reduce.gather()
    gram_ref[...] = reduce.finish()
    for copy in stores:
        copy.wait()


def normalise(state, inverse):
    return pl.pallas_call(
        normalise_kernel,
        out_shape=(jax.ShapeDtypeStruct(state.shape, F32), jax.ShapeDtypeStruct((MODES, MODES), F32)),
        in_specs=[ANY, VMEM],
        out_specs=(ANY, VMEM),
        scratch_shapes=[
            vmem(*state.shape), vmem(128, 256), *REDUCE_SCRATCH, pltpu.SemaphoreType.DMA((6,)), pltpu.SemaphoreType.DMA((8,))
        ],
        compiler_params=pltpu.CompilerParams(collective_id=1, has_side_effects=True, vmem_limit_bytes=16 * 2**20),
        name="normalise",
    )(state, inverse)


def factor(gram_blocks):
    sub = lax.broadcasted_iota(jnp.int32, (8, 128), 0)
    lane = lax.broadcasted_iota(jnp.int32, (8, 128), 1)
    w = list(gram_blocks)
    for k in range(MODES):
        b, s = divmod(k, 8)
        panel = w[b]
        column = jnp.broadcast_to(panel[:, k : k + 1], (8, 128))
        scale = jnp.broadcast_to((1.0 / column)[s : s + 1, :], (8, 128))
        here = lane == k
        pivot = jnp.where(here, scale, jnp.broadcast_to(panel[s : s + 1, :], (8, 128)) * scale)
        for j in range(b, 16):
            c = column if j == b else jnp.broadcast_to(w[j][:, k : k + 1], (8, 128))
            new = jnp.where(here, 0.0, w[j]) - c * pivot
            w[j] = jnp.where(sub > s, new, w[j]) if j == b else new
    diagonal = jnp.zeros((8, 128), F32)
    inverse = []
    for i in range(16):
        on = lane == sub + 8 * i
        pivots = jnp.where(on, w[i], 0.0)
        diagonal = diagonal + pivots
        root = lax.rsqrt(jnp.sum(pivots, axis=1, keepdims=True))
        inverse.append(jnp.where(lane < sub + 8 * i, w[i], jnp.where(on, 1.0, 0.0)) * root)
    return inverse, 0.5 * jnp.log(jnp.sum(diagonal, axis=0, keepdims=True))


def factor_kernel(gram_ref, inverse_ref, log_ref):
    inverse, logs = factor([gram_ref[8 * i : 8 * i + 8, :] for i in range(16)])
    for i in range(16):
        inverse_ref[8 * i : 8 * i + 8, :] = inverse[i]
    log_ref[...] = logs


def factorise(gram):
    return pl.pallas_call(
        factor_kernel,
        out_shape=(jax.ShapeDtypeStruct((MODES, MODES), F32), jax.ShapeDtypeStruct((1, MODES), F32)),
        name="factorise",
    )(gram)


def finish_kernel(b_ref, inverse_ref, out_ref):
    weights = weights_of(inverse_ref[...])

    @pl.loop(0, b_ref.shape[0] // 256)
    def _(j):
        here = pl.ds(pl.multiple_of(256 * j, 256), 256)
        out_ref[here, :] = apply_inverse(b_ref[here, :], weights)


def finish(state, inverse):
    rows = 768
    return pl.pallas_call(
        finish_kernel,
        out_shape=jax.ShapeDtypeStruct(state.shape, F32),
        grid=(state.shape[0] // rows,),
        in_specs=[pl.BlockSpec((rows, MODES), lambda i: (i, 0)), pl.BlockSpec((MODES, MODES), lambda i: (0, 0))],
        out_specs=pl.BlockSpec((rows, MODES), lambda i: (i, 0)),
        name="finish",
    )(state, inverse)


def body(tangents, sea_mask, levels, current):
    state, gram = start(tangents, sea_mask, levels, current)
    inverse, logs = factorise(gram)
    state, gram = normalise(state.reshape(-1, MODES), inverse)
    inverse, more = factorise(gram)
    out = finish(state, inverse)
    return out.reshape(tangents.shape), (logs + more)[0]


def solution(mesh):
    placed = (P(None, "row", "col", None), P("row", "col"), P("row", "col"), P("row", "col"))
    return jax.shard_map(
        body,
        mesh=mesh,
        in_specs=placed,
        out_specs=(P(None, "row", "col", None), P()),
        check_vma=False,
    )
```

```python
import jax
import jax.numpy as jnp
from jax import lax
from jax.experimental import pallas as pl
from jax.experimental.pallas import tpu as pltpu
from jax.sharding import PartitionSpec as P

MESH = pl.DeviceIdType.MESH
F32 = jnp.float32
BF16 = jnp.bfloat16
ROWS, COLS = 8, 16
LAT, LON, MODES = 64, 32, 128
LEVELS = 50
CELLS = 512 * 512
ANY = pl.BlockSpec(memory_space=pl.ANY)
VMEM = pl.BlockSpec(memory_space=pltpu.VMEM)


def vmem(*shape):
    return pltpu.VMEM(shape, F32)


def remote(src, dst, sems, k, dev):
    return pltpu.make_async_remote_copy(
        src_ref=src, dst_ref=dst, send_sem=sems.at[2 * k], recv_sem=sems.at[2 * k + 1], device_id=dev, device_id_type=MESH
    )


def at(row, col):
    return {"row": row, "col": col}


def shift(row, col, drow, dcol):
    return at(lax.rem(row + drow + ROWS, ROWS), lax.rem(col + dcol + COLS, COLS))


def inner_peer(row, col, d):
    member = lax.rem(lax.rem(col, 8) + d, 8)
    return member, at(row, (col // 8) * 8 + member)


def outer_index(row, col):
    return (col // 8) * 8 + row


def outer_peer(row, col, d):
    k = lax.rem(outer_index(row, col) + d, 16)
    return at(lax.rem(k, 8), (k // 8) * 8 + lax.rem(col, 8))


NEIGHBOURS = [(0, -1), (0, 1), (-1, 0), (1, 0), (-1, -1), (-1, 1), (1, -1), (1, 1)]


def greet(row, col):
    barrier = pltpu.get_barrier_semaphore()
    peers = [inner_peer(row, col, d)[1] for d in range(1, 8)] + [outer_peer(row, col, d) for d in range(1, 16)]
    peers += [shift(row, col, a, b) for a, b in NEIGHBOURS]
    for dev in peers:
        pl.semaphore_signal(barrier, inc=1, device_id=dev, device_id_type=MESH)
    return lambda: pl.semaphore_wait(barrier, len(peers))


class Reduce:
    def __init__(self, row, col, g, inner, part, outer, total, sems):
        self.row, self.col = row, col
        self.g, self.inner, self.part, self.outer, self.total, self.sems = g, inner, part, outer, total, sems
        self.me = lax.rem(col, 8)
        self.waits = []

    def scatter(self):
        for d in range(1, 8):
            member, dev = inner_peer(self.row, self.col, d)
            remote(self.g.at[member], self.inner.at[d], self.sems, 0, dev).start()

    def exchange(self):
        w = remote(self.inner.at[pl.ds(1, 7)], self.inner.at[pl.ds(1, 7)], self.sems, 0, inner_peer(self.row, self.col, 1)[1])
        w.wait_recv()
        s = self.g[self.me]
        for d in range(1, 8):
            s = s + self.inner[d]
        self.part[...] = s
        k = outer_index(self.row, self.col)
        for d in range(1, 16):
            remote(self.part, self.outer.at[k], self.sems, 1, outer_peer(self.row, self.col, d)).start()
        self.outer[k] = s
        self.waits.append(w)

    def gather(self):
        w = remote(self.outer.at[pl.ds(0, 15)], self.outer.at[pl.ds(0, 15)], self.sems, 1, outer_peer(self.row, self.col, 1))
        w.wait_recv()
        t = self.outer[0]
        for e in range(1, 16):
            t = t + self.outer[e]
        self.total[self.me] = t
        for d in range(1, 8):
            remote(self.total.at[self.me], self.total.at[self.me], self.sems, 2, inner_peer(self.row, self.col, d)[1]).start()
        self.waits.append(w)

    def finish(self):
        w = remote(self.total.at[pl.ds(0, 7)], self.total.at[pl.ds(0, 7)], self.sems, 2, inner_peer(self.row, self.col, 1)[1])
        w.wait_recv()
        self.waits.append(w)
        for w in self.waits:
            w.wait_send()
        return self.total[...].reshape(MODES, MODES)


REDUCE_SCRATCH = [vmem(8, 16, 128), vmem(8, 16, 128), vmem(16, 128), vmem(16, 16, 128), vmem(8, 16, 128)]


def split(x):
    hi = x.astype(BF16)
    return hi, (x - hi.astype(F32)).astype(BF16)


def gram_of(x):
    hi, lo = split(x)
    return lax.dot_general(hi, jnp.concatenate([hi, lo], axis=1), (((0,), (0,)), ((), ())), preferred_element_type=F32)


def close_gram(acc):
    cross = acc[:, 128:]
    return (acc[:, :128] + cross + cross.T) * (1.0 / CELLS)


def weights_of(inverse):
    hi, lo = split(inverse)
    return jnp.concatenate(
        [jnp.concatenate([hi, hi], axis=1), jnp.concatenate([lo, jnp.zeros_like(lo)], axis=1)], axis=0
    )


def apply_inverse(x, weights):
    hi, lo = split(x)
    both = lax.dot_general(
        jnp.concatenate([hi, lo], axis=1), weights, (((1,), (1,)), ((), ())), preferred_element_type=F32
    )
    return both[:, :128] + both[:, 128:]


def lanes(x, k):
    return jnp.broadcast_to(x[:, k : k + 1], (8, 128))


def sublanes(x, s):
    return jnp.broadcast_to(x[s : s + 1, :], (8, 128))


def factor(blocks):
    sub = lax.broadcasted_iota(jnp.int32, (8, 128), 0)
    lane = lax.broadcasted_iota(jnp.int32, (8, 128), 1)
    below = [sub > s for s in range(8)]
    w = list(blocks)
    for b in range(16):
        inside = (lane >= 8 * b) & (lane < 8 * b + 8)
        p = w[b]
        c = [lanes(p, 8 * b + m) for m in range(8)]
        upper, scales, pivot_rows = {}, [], []
        for s in range(8):
            here = lane == 8 * b + s
            scale = sublanes(1.0 / c[s], s)
            column = jnp.where(below[s], c[s], 0.0)
            for m in range(s + 1, 8):
                upper[s, m] = sublanes(c[m], s)
            for m in range(s + 1, 8):
                c[m] = c[m] - column * (scale * upper[s, m])
            row = jnp.where(here, 1.0, sublanes(p, s))
            if s < 7:
                p = jnp.where(here & below[s], 0.0, p) - column * (scale * row)
            scales.append(scale)
            pivot_rows.append(jnp.where(inside & (lane > 8 * b + s), 0.0, row))
        w[b] = p
        for j in range(b + 1, 16):
            a = [lanes(w[j], 8 * b + m) for m in range(8)]
            t = jnp.where(inside, 0.0, w[j])
            for s in range(8):
                multiplier = a[s] * scales[s]
                for m in range(s + 1, 8):
                    a[m] = a[m] - multiplier * upper[s, m]
                t = t - multiplier * pivot_rows[s]
            w[j] = t
    diagonal = jnp.zeros((8, 128), F32)
    inverse = []
    for i in range(16):
        on = lane == sub + 8 * i
        pivots = jnp.where(on, w[i], 0.0)
        diagonal = diagonal + pivots
        root = lax.rsqrt(jnp.sum(pivots, axis=1, keepdims=True))
        inverse.append(jnp.where(lane < sub + 8 * i, w[i], jnp.where(on, 1.0, 0.0)) * root)
    return jnp.concatenate(inverse, axis=0), 0.5 * jnp.log(jnp.sum(diagonal, axis=0, keepdims=True))


def model_step(src, src_row, dst, dst_row, planes, spin, plane_row, rows, starts):
    @pl.loop(0, rows)
    def _(i):
        r, p, o = src_row + i, plane_row + i, dst_row + i
        cor = jnp.broadcast_to(spin[pl.ds(p, 1), :], (8, 128))
        for s in starts:
            here = pl.ds(s, 8)
            sea, flow, deep = planes[0, p, here, :], planes[1, p, here, :], planes[2, p, here, :]
            mid = [src[q, r, here, :] for q in range(3)]
            east = [src[q, r, pl.ds(s + 1, 8), :] for q in range(3)]
            west = [src[q, r, pl.ds(s - 1, 8), :] for q in range(3)]
            north = [src[q, r + 1, here, :] for q in range(3)]
            south = [src[q, r - 1, here, :] for q in range(3)]
            along = [east[q] - west[q] for q in range(3)]
            moved = [
                0.4 * mid[q] + 0.15 * ((east[q] + west[q]) + (north[q] + south[q])) - flow * along[q] for q in range(3)
            ]
            dst[0, o, here, :] = sea * (moved[0] - 0.25 * along[2] + cor * mid[1])
            dst[1, o, here, :] = sea * (moved[1] - 0.25 * (north[2] - south[2]) - cor * mid[0])
            dst[2, o, here, :] = sea * (moved[2] - deep * (along[0] + (north[1] - south[1])))


OUTER_STARTS = (7, 15, 23, 31, 39)
INNER_STARTS = (8, 16, 24, 32)


def start_kernel(
    x_hbm, mask_ref, levels_ref, current_ref, b_hbm, gram_ref, logs_ref,
    x, y, planes, table, north_table, south_table, spin, acc,
    send_w, send_e, recv_w, recv_e, send_k, recv_k, ghost,
    b, g, inner, part, outer, total, sems, g2, inner2, part2, outer2, total2, sems2, hsems, lsem,
):
    row, col = lax.axis_index("row"), lax.axis_index("col")
    load = pltpu.make_async_copy(x_hbm, x.at[:, pl.ds(2, LAT), pl.ds(8, LON), :], lsem.at[0])
    load.start()
    wait_barrier = greet(row, col)

    packed = jnp.concatenate(
        [
            mask_ref[...].astype(F32),
            0.5 * current_ref[...],
            0.5 * ((levels_ref[...] + 1).astype(F32) / LEVELS),
            jnp.zeros((LAT, 32), F32),
        ],
        axis=1,
    )
    turned = jnp.concatenate([packed, jnp.zeros((64, 128), F32)], axis=0).T
    for k in range(3):
        table[k, 8:40, :] = turned[32 * k : 32 * k + 32, :]
    lat = lax.broadcasted_iota(jnp.int32, (72, 128), 0) + row * LAT - 1
    angle = (-70.0 + 140.0 * (lat.astype(F32) + 0.5) / (ROWS * LAT)) * (jnp.pi / 180.0)
    spin[...] = 0.4 * jnp.sin(angle)

    def row_copies(e, src, off, k):
        width = slice(None) if off == 0 else pl.ds(8, LON)
        return [
            remote(src.at[:, pl.ds(off, 2), width, :], ghost.at[e, 1], hsems, k, shift(row, col, -1, 0)),
            remote(src.at[:, pl.ds(off + 62, 2), width, :], ghost.at[e, 0], hsems, k + 1, shift(row, col, 1, 0)),
        ]

    def pack():
        @pl.loop(0, 16)
        def _(j):
            for q in range(3):
                for m in range(4):
                    send_w[q, j, 2 * m : 2 * m + 2, :] = x[q, 4 * j + m + 2, 8:10, :]
                    send_e[q, j, 2 * m : 2 * m + 2, :] = x[q, 4 * j + m + 2, 38:40, :]

        for c, (i, j) in enumerate(((2, 8), (2, 39), (65, 8), (65, 39))):
            for q in range(3):
                send_k[c, q : q + 1, :] = x[q, i, j : j + 1, :]

    def side_copies(e, k):
        out = [
            remote(send_w, recv_e.at[e], hsems, k, shift(row, col, 0, -1)),
            remote(send_e, recv_w.at[e], hsems, k + 1, shift(row, col, 0, 1)),
        ]
        for c, (a, b) in enumerate(((-1, -1), (-1, 1), (1, -1), (1, 1))):
            out.append(remote(send_k.at[c], recv_k.at[e, 3 - c], hsems, k + 2 + c, shift(row, col, a, b)))
        return out

    def unpack(e):
        @pl.loop(0, 16)
        def _(j):
            for q in range(3):
                for m in range(4):
                    x[q, 4 * j + m + 2, 6:8, :] = recv_w[e, q, j, 2 * m : 2 * m + 2, :]
                    x[q, 4 * j + m + 2, 40:42, :] = recv_e[e, q, j, 2 * m : 2 * m + 2, :]

        for c, (i, j) in enumerate(((1, 7), (1, 40), (66, 7), (66, 40))):
            for q in range(3):
                x[q, i, j : j + 1, :] = recv_k[e, c, q : q + 1, :]

        x[:, 0:2, 8:40, :] = ghost[e, 0]
        x[:, 66:68, 8:40, :] = ghost[e, 1]

        @pl.when(row == 0)
        def _():
            x[:, 0:2, :, :] = jnp.zeros((3, 2, 48, 128), F32)

        @pl.when(row == ROWS - 1)
        def _():
            x[:, 66:68, :, :] = jnp.zeros((3, 2, 48, 128), F32)

    wait_barrier()
    tables = [
        remote(table.at[:, pl.ds(8, 8), :], table.at[:, pl.ds(40, 8), :], hsems, 8, shift(row, col, 0, -1)),
        remote(table.at[:, pl.ds(32, 8), :], table.at[:, pl.ds(0, 8), :], hsems, 9, shift(row, col, 0, 1)),
        remote(table.at[:, pl.ds(8, 32), :], north_table, hsems, 10, shift(row, col, -1, 0)),
        remote(table.at[:, pl.ds(8, 32), :], south_table, hsems, 11, shift(row, col, 1, 0)),
    ]
    first = row_copies(0, x_hbm, 0, 0)
    for copy in tables + first:
        copy.start()
    load.wait()
    pack()
    sides = side_copies(0, 2)
    for copy in sides:
        copy.start()

    def spread(k, tile):
        start = pl.multiple_of(8 * tile, 8)
        lanes = table[k, pl.ds(start, 8), :]
        for i in range(LAT):
            planes[k, i + 1, pl.ds(start, 8), :] = jnp.broadcast_to(lanes[:, i : i + 1], (8, 128))

    for k in range(3):
        @pl.loop(1, 5)
        def _(tile):
            spread(k, tile)

    for copy in tables:
        copy.wait()
    for k in range(3):
        @pl.loop(0, 2)
        def _(edge):
            spread(k, 5 * edge)

        for tile in range(4):
            planes[k, 65, 8 * tile + 8 : 8 * tile + 16, :] = jnp.broadcast_to(north_table[k, 8 * tile : 8 * tile + 8, 0:1], (8, 128))
            planes[k, 0, 8 * tile + 8 : 8 * tile + 16, :] = jnp.broadcast_to(south_table[k, 8 * tile : 8 * tile + 8, 63:64], (8, 128))

    @pl.when(row == 0)
    def _():
        planes[0, 0, :, :] = jnp.zeros((48, 128), F32)

    @pl.when(row == ROWS - 1)
    def _():
        planes[0, 65, :, :] = jnp.zeros((48, 128), F32)

    for copy in first + sides:
        copy.wait()
    unpack(0)
    model_step(x, 1, y, 0, planes, spin, 0, LAT + 2, OUTER_STARTS)
    model_step(y, 1, x, 2, planes, spin, 1, LAT, INNER_STARTS)

    def chunk(h):
        return jnp.concatenate([x[q, pl.ds(32 * h + 2, 32), 8:40, :].reshape(1024, MODES) for q in range(3)], axis=0)

    acc[...] = jnp.zeros_like(acc)

    @pl.loop(0, 2)
    def _(h):
        acc[...] += gram_of(chunk(h))

    g[...] = close_gram(acc[...]).reshape(8, 16, 128)
    reduce = Reduce(row, col, g, inner, part, outer, total, sems)
    reduce.scatter()
    pack()
    halo = row_copies(1, x, 2, 12) + side_copies(1, 14)
    for copy in halo:
        copy.start()
    reduce.exchange()
    for copy in halo:
        copy.wait()
    unpack(1)
    model_step(x, 1, y, 0, planes, spin, 0, LAT + 2, OUTER_STARTS)
    reduce.gather()
    model_step(y, 1, x, 2, planes, spin, 1, LAT, INNER_STARTS)
    gram = reduce.finish()

    inverse, logs = factor([gram[8 * i : 8 * i + 8, :] for i in range(16)])
    logs_ref[...] = logs
    weights = weights_of(inverse)
    acc[...] = jnp.zeros_like(acc)

    @pl.loop(0, 2)
    def _(h):
        normal = apply_inverse(chunk(h), weights)
        for q in range(3):
            b[q, pl.ds(32 * h, 32), :, :] = normal[1024 * q : 1024 * q + 1024, :].reshape(32, LON, MODES)
        acc[...] += gram_of(normal)

    store = pltpu.make_async_copy(b, b_hbm, lsem.at[0])
    store.start()
    g2[...] = close_gram(acc[...]).reshape(8, 16, 128)
    second = Reduce(row, col, g2, inner2, part2, outer2, total2, sems2)
    second.scatter()
    second.exchange()
    second.gather()
    gram_ref[...] = second.finish()
    store.wait()


def start(tangents, sea_mask, levels, current):
    return pl.pallas_call(
        start_kernel,
        out_shape=(
            jax.ShapeDtypeStruct(tangents.shape, F32),
            jax.ShapeDtypeStruct((MODES, MODES), F32),
            jax.ShapeDtypeStruct((1, MODES), F32),
        ),
        in_specs=[ANY, VMEM, VMEM, VMEM],
        out_specs=(ANY, VMEM, VMEM),
        scratch_shapes=[
            vmem(3, 68, 48, 128), vmem(3, 66, 48, 128), vmem(3, 66, 48, 128), vmem(3, 48, 128), vmem(3, 32, 128),
            vmem(3, 32, 128), vmem(72, 128), vmem(128, 256),
            vmem(3, 16, 8, 128), vmem(3, 16, 8, 128), vmem(2, 3, 16, 8, 128), vmem(2, 3, 16, 8, 128), vmem(4, 8, 128), vmem(2, 4, 8, 128),
            vmem(2, 2, 3, 2, LON, 128),
            vmem(3, LAT, LON, MODES),
            *REDUCE_SCRATCH, pltpu.SemaphoreType.DMA((6,)),
            *REDUCE_SCRATCH, pltpu.SemaphoreType.DMA((6,)),
            pltpu.SemaphoreType.DMA((40,)), pltpu.SemaphoreType.DMA((1,)),
        ],
        compiler_params=pltpu.CompilerParams(collective_id=0, has_side_effects=True, vmem_limit_bytes=48 * 2**20),
        name="start",
    )(tangents, sea_mask, levels, current)


def finish_kernel(b_ref, gram_ref, logs_ref, out_ref, growth_ref, weights):
    @pl.when(pl.program_id(0) == 0)
    def _():
        inverse, logs = factor([gram_ref[8 * i : 8 * i + 8, :] for i in range(16)])
        weights[...] = weights_of(inverse)
        growth_ref[...] = logs_ref[...] + logs

    out_ref[...] = apply_inverse(b_ref[...], weights[...])


def finish(state, gram, logs):
    rows = 1536
    whole = lambda i: (0, 0)
    return pl.pallas_call(
        finish_kernel,
        out_shape=(jax.ShapeDtypeStruct(state.shape, F32), jax.ShapeDtypeStruct((1, MODES), F32)),
        grid=(state.shape[0] // rows,),
        in_specs=[
            pl.BlockSpec((rows, MODES), lambda i: (i, 0)), pl.BlockSpec((MODES, MODES), whole), pl.BlockSpec((1, MODES), whole)
        ],
        out_specs=(pl.BlockSpec((rows, MODES), lambda i: (i, 0)), pl.BlockSpec((1, MODES), whole)),
        scratch_shapes=[pltpu.VMEM((2 * MODES, 2 * MODES), BF16)],
        name="finish",
    )(state, gram, logs)


def body(tangents, sea_mask, levels, current):
    state, gram, logs = start(tangents, sea_mask, levels, current)
    out, growth = finish(state.reshape(-1, MODES), gram, logs)
    return out.reshape(tangents.shape), growth[0]


def solution(mesh):
    placed = (P(None, "row", "col", None), P("row", "col"), P("row", "col"), P("row", "col"))
    return jax.shard_map(
        body,
        mesh=mesh,
        in_specs=placed,
        out_specs=(P(None, "row", "col", None), P()),
        check_vma=False,
    )
```

```python
import jax
import jax.numpy as jnp
from jax import lax
from jax.experimental import pallas as pl
from jax.experimental.pallas import tpu as pltpu
from jax.sharding import PartitionSpec as P

MESH = pl.DeviceIdType.MESH
F32 = jnp.float32
BF16 = jnp.bfloat16
ROWS, COLS = 8, 16
LAT, LON, MODES = 64, 32, 128
LEVELS = 50
CELLS = 512 * 512
ANY = pl.BlockSpec(memory_space=pl.ANY)
VMEM = pl.BlockSpec(memory_space=pltpu.VMEM)
HBM = pl.BlockSpec(memory_space=pltpu.HBM)


def vmem(*shape):
    return pltpu.VMEM(shape, F32)


def remote(src, dst, sems, k, dev):
    return pltpu.make_async_remote_copy(
        src_ref=src, dst_ref=dst, send_sem=sems.at[2 * k], recv_sem=sems.at[2 * k + 1], device_id=dev, device_id_type=MESH
    )


def at(row, col):
    return {"row": row, "col": col}


def shift(row, col, drow, dcol):
    return at(lax.rem(row + drow + ROWS, ROWS), lax.rem(col + dcol + COLS, COLS))


def inner_peer(row, col, d):
    member = lax.rem(lax.rem(col, 8) + d, 8)
    return member, at(row, (col // 8) * 8 + member)


def outer_index(row, col):
    return (col // 8) * 8 + row


def outer_peer(row, col, d):
    k = lax.rem(outer_index(row, col) + d, 16)
    return at(lax.rem(k, 8), (k // 8) * 8 + lax.rem(col, 8))


NEIGHBOURS = [(0, -1), (0, 1), (-1, 0), (1, 0), (-1, -1), (-1, 1), (1, -1), (1, 1)]


def greet(row, col):
    barrier = pltpu.get_barrier_semaphore()
    peers = [inner_peer(row, col, d)[1] for d in range(1, 8)] + [outer_peer(row, col, d) for d in range(1, 16)]
    peers += [shift(row, col, a, b) for a, b in NEIGHBOURS]
    for dev in peers:
        pl.semaphore_signal(barrier, inc=1, device_id=dev, device_id_type=MESH)
    return lambda: pl.semaphore_wait(barrier, len(peers))


class Reduce:
    def __init__(self, row, col, g, inner, part, outer, total, sems):
        self.row, self.col = row, col
        self.g, self.inner, self.part, self.outer, self.total, self.sems = g, inner, part, outer, total, sems
        self.me = lax.rem(col, 8)
        self.waits = []

    def scatter(self):
        for d in range(1, 8):
            member, dev = inner_peer(self.row, self.col, d)
            remote(self.g.at[member], self.inner.at[d], self.sems, 0, dev).start()

    def exchange(self):
        w = remote(self.inner.at[pl.ds(1, 7)], self.inner.at[pl.ds(1, 7)], self.sems, 0, inner_peer(self.row, self.col, 1)[1])
        w.wait_recv()
        s = self.g[self.me]
        for d in range(1, 8):
            s = s + self.inner[d]
        self.part[...] = s
        k = outer_index(self.row, self.col)
        for d in range(1, 16):
            remote(self.part, self.outer.at[k], self.sems, 1, outer_peer(self.row, self.col, d)).start()
        self.outer[k] = s
        self.waits.append(w)

    def gather(self):
        w = remote(self.outer.at[pl.ds(0, 15)], self.outer.at[pl.ds(0, 15)], self.sems, 1, outer_peer(self.row, self.col, 1))
        w.wait_recv()
        t = self.outer[0]
        for e in range(1, 16):
            t = t + self.outer[e]
        self.total[self.me] = t
        for d in range(1, 8):
            remote(self.total.at[self.me], self.total.at[self.me], self.sems, 2, inner_peer(self.row, self.col, d)[1]).start()
        self.waits.append(w)

    def finish(self):
        w = remote(self.total.at[pl.ds(0, 7)], self.total.at[pl.ds(0, 7)], self.sems, 2, inner_peer(self.row, self.col, 1)[1])
        w.wait_recv()
        self.waits.append(w)
        for w in self.waits:
            w.wait_send()
        return self.total[...].reshape(MODES, MODES)


REDUCE_SCRATCH = [vmem(8, 16, 128), vmem(8, 16, 128), vmem(16, 128), vmem(16, 16, 128), vmem(8, 16, 128)]


def split(x):
    hi = x.astype(BF16)
    return hi, (x - hi.astype(F32)).astype(BF16)


def gram_of(x):
    hi, lo = split(x)
    return lax.dot_general(hi, jnp.concatenate([hi, lo], axis=1), (((0,), (0,)), ((), ())), preferred_element_type=F32)


def close_gram(acc):
    cross = acc[:, 128:]
    return (acc[:, :128] + cross + cross.T) * (1.0 / CELLS)


def weights_of(inverse):
    hi, lo = split(inverse)
    return jnp.concatenate(
        [jnp.concatenate([hi, hi], axis=1), jnp.concatenate([lo, jnp.zeros_like(lo)], axis=1)], axis=0
    )


def apply_inverse(x, weights):
    hi, lo = split(x)
    both = lax.dot_general(
        jnp.concatenate([hi, lo], axis=1), weights, (((1,), (1,)), ((), ())), preferred_element_type=F32
    )
    return both[:, :128] + both[:, 128:]


def lanes(x, k):
    return jnp.broadcast_to(x[:, k : k + 1], (8, 128))


def sublanes(x, s):
    return jnp.broadcast_to(x[s : s + 1, :], (8, 128))


def factor(blocks):
    sub = lax.broadcasted_iota(jnp.int32, (8, 128), 0)
    lane = lax.broadcasted_iota(jnp.int32, (8, 128), 1)
    below = [sub > s for s in range(8)]
    w = list(blocks)
    for b in range(16):
        inside = (lane >= 8 * b) & (lane < 8 * b + 8)
        p = w[b]
        c = [lanes(p, 8 * b + m) for m in range(8)]
        upper, scales, pivot_rows = {}, [], []
        for s in range(8):
            here = lane == 8 * b + s
            scale = sublanes(1.0 / c[s], s)
            column = jnp.where(below[s], c[s], 0.0)
            for m in range(s + 1, 8):
                upper[s, m] = sublanes(c[m], s)
            for m in range(s + 1, 8):
                c[m] = c[m] - column * (scale * upper[s, m])
            row = jnp.where(here, 1.0, sublanes(p, s))
            if s < 7:
                p = jnp.where(here & below[s], 0.0, p) - column * (scale * row)
            scales.append(scale)
            pivot_rows.append(jnp.where(inside & (lane > 8 * b + s), 0.0, row))
        w[b] = p
        for j in range(b + 1, 16):
            a = [lanes(w[j], 8 * b + m) for m in range(8)]
            t = jnp.where(inside, 0.0, w[j])
            for s in range(8):
                multiplier = a[s] * scales[s]
                for m in range(s + 1, 8):
                    a[m] = a[m] - multiplier * upper[s, m]
                t = t - multiplier * pivot_rows[s]
            w[j] = t
    diagonal = jnp.zeros((8, 128), F32)
    inverse = []
    for i in range(16):
        on = lane == sub + 8 * i
        pivots = jnp.where(on, w[i], 0.0)
        diagonal = diagonal + pivots
        root = lax.rsqrt(jnp.sum(pivots, axis=1, keepdims=True))
        inverse.append(jnp.where(lane < sub + 8 * i, w[i], jnp.where(on, 1.0, 0.0)) * root)
    return jnp.concatenate(inverse, axis=0), 0.5 * jnp.log(jnp.sum(diagonal, axis=0, keepdims=True))


def model_step(src, src_row, dst, dst_row, planes, spin, count, lat_of, starts):
    @pl.loop(0, count)
    def _(i):
        lat = lat_of(i)
        r, p, o = src_row + lat, 1 + lat, dst_row + lat
        cor = jnp.broadcast_to(spin[pl.ds(p, 1), :], (8, 128))
        for s in starts:
            here = pl.ds(s, 8)
            sea, flow, deep = planes[0, p, here, :], planes[1, p, here, :], planes[2, p, here, :]
            mid = [src[q, r, here, :] for q in range(3)]
            east = [src[q, r, pl.ds(s + 1, 8), :] for q in range(3)]
            west = [src[q, r, pl.ds(s - 1, 8), :] for q in range(3)]
            north = [src[q, r + 1, here, :] for q in range(3)]
            south = [src[q, r - 1, here, :] for q in range(3)]
            along = [east[q] - west[q] for q in range(3)]
            moved = [
                0.4 * mid[q] + 0.15 * ((east[q] + west[q]) + (north[q] + south[q])) - flow * along[q] for q in range(3)
            ]
            dst[0, o, here, :] = sea * (moved[0] - 0.25 * along[2] + cor * mid[1])
            dst[1, o, here, :] = sea * (moved[1] - 0.25 * (north[2] - south[2]) - cor * mid[0])
            dst[2, o, here, :] = sea * (moved[2] - deep * (along[0] + (north[1] - south[1])))


OUTER_STARTS = (7, 15, 23, 31, 39)
INNER_STARTS = (8, 16, 24, 32)


def start_kernel(
    x_hbm, fields_ref, b, gram_ref, logs_ref,
    x, y, z, planes, table, north_table, south_table, spin, acc,
    send_w, send_e, recv_w, recv_e, send_k, recv_k, ghost,
    g, inner, part, outer, total, sems, g2, inner2, part2, outer2, total2, sems2, hsems, lsem,
):
    row, col = lax.axis_index("row"), lax.axis_index("col")
    load = pltpu.make_async_copy(x_hbm, x.at[:, pl.ds(2, LAT), pl.ds(8, LON), :], lsem.at[0])
    load.start()
    wait_barrier = greet(row, col)

    table[:, 8:40, 0:LAT] = fields_ref[...]
    lat = lax.broadcasted_iota(jnp.int32, (72, 128), 0) + row * LAT - 1
    angle = (-70.0 + 140.0 * (lat.astype(F32) + 0.5) / (ROWS * LAT)) * (jnp.pi / 180.0)
    spin[...] = 0.4 * jnp.sin(angle)

    def row_copies(e, src, off, k):
        width = slice(None) if off == 0 else pl.ds(8, LON)
        return [
            remote(src.at[:, pl.ds(off, 2), width, :], ghost.at[e, 1], hsems, k, shift(row, col, -1, 0)),
            remote(src.at[:, pl.ds(off + 62, 2), width, :], ghost.at[e, 0], hsems, k + 1, shift(row, col, 1, 0)),
        ]

    def pack(x):
        @pl.loop(0, 16)
        def _(j):
            for q in range(3):
                for m in range(4):
                    send_w[q, j, 2 * m : 2 * m + 2, :] = x[q, 4 * j + m + 2, 8:10, :]
                    send_e[q, j, 2 * m : 2 * m + 2, :] = x[q, 4 * j + m + 2, 38:40, :]

        for c, (i, j) in enumerate(((2, 8), (2, 39), (65, 8), (65, 39))):
            for q in range(3):
                send_k[c, q : q + 1, :] = x[q, i, j : j + 1, :]

    def side_copies(e, k):
        out = [
            remote(send_w, recv_e.at[e], hsems, k, shift(row, col, 0, -1)),
            remote(send_e, recv_w.at[e], hsems, k + 1, shift(row, col, 0, 1)),
        ]
        for c, (a, b) in enumerate(((-1, -1), (-1, 1), (1, -1), (1, 1))):
            out.append(remote(send_k.at[c], recv_k.at[e, 3 - c], hsems, k + 2 + c, shift(row, col, a, b)))
        return out

    def unpack_sides(e, x):
        @pl.loop(0, 16)
        def _(j):
            for q in range(3):
                for m in range(4):
                    x[q, 4 * j + m + 2, 6:8, :] = recv_w[e, q, j, 2 * m : 2 * m + 2, :]
                    x[q, 4 * j + m + 2, 40:42, :] = recv_e[e, q, j, 2 * m : 2 * m + 2, :]

    def unpack_rows(e, x):
        for c, (i, j) in enumerate(((1, 7), (1, 40), (66, 7), (66, 40))):
            for q in range(3):
                x[q, i, j : j + 1, :] = recv_k[e, c, q : q + 1, :]

        x[:, 0:2, 8:40, :] = ghost[e, 0]
        x[:, 66:68, 8:40, :] = ghost[e, 1]

        @pl.when(row == 0)
        def _():
            x[:, 0:2, :, :] = jnp.zeros((3, 2, 48, 128), F32)

        @pl.when(row == ROWS - 1)
        def _():
            x[:, 66:68, :, :] = jnp.zeros((3, 2, 48, 128), F32)

    def spread(k, tile):
        start = pl.multiple_of(8 * tile, 8)
        lanes = table[k, pl.ds(start, 8), :]
        for i in range(LAT):
            planes[k, i + 1, pl.ds(start, 8), :] = jnp.broadcast_to(lanes[:, i : i + 1], (8, 128))

    def chunk(x, h):
        return jnp.concatenate([x[q, pl.ds(32 * h + 2, 32), 8:40, :].reshape(1024, MODES) for q in range(3)], axis=0)

    def inside(x, z):
        model_step(x, 2, y, 1, planes, spin, LAT - 2, lambda i: i + 1, INNER_STARTS)
        model_step(y, 1, z, 2, planes, spin, LAT - 4, lambda i: i + 2, INNER_STARTS)

    def side_edges(x):
        model_step(x, 2, y, 1, planes, spin, LAT - 2, lambda i: i + 1, (7, 33))

    def other_edges(x, z):
        model_step(x, 2, y, 1, planes, spin, 4, lambda i: i - 1 + 62 * (i // 2), OUTER_STARTS)
        model_step(y, 1, z, 2, planes, spin, 4, lambda i: i + 60 * (i // 2), INNER_STARTS)
        model_step(y, 1, z, 2, planes, spin, LAT - 4, lambda i: i + 2, (8, 32))

    rows = row_copies(0, x_hbm, 0, 0)
    sides = side_copies(0, 2)
    tables = [
        remote(table.at[:, pl.ds(8, 8), :], table.at[:, pl.ds(40, 8), :], hsems, 8, shift(row, col, 0, -1)),
        remote(table.at[:, pl.ds(32, 8), :], table.at[:, pl.ds(0, 8), :], hsems, 9, shift(row, col, 0, 1)),
        remote(table.at[:, pl.ds(8, 32), :], north_table, hsems, 10, shift(row, col, -1, 0)),
        remote(table.at[:, pl.ds(8, 32), :], south_table, hsems, 11, shift(row, col, 1, 0)),
    ]
    for k in range(3):
        @pl.loop(1, 5)
        def _(tile):
            spread(k, tile)

    load.wait()
    pack(x)
    wait_barrier()
    for copy in sides + tables + rows:
        copy.start()
    inside(x, z)
    for copy in tables:
        copy.wait()
    for k in range(3):
        @pl.loop(0, 2)
        def _(edge):
            spread(k, 5 * edge)

        for tile in range(4):
            planes[k, 65, 8 * tile + 8 : 8 * tile + 16, :] = jnp.broadcast_to(north_table[k, 8 * tile : 8 * tile + 8, 0:1], (8, 128))
            planes[k, 0, 8 * tile + 8 : 8 * tile + 16, :] = jnp.broadcast_to(south_table[k, 8 * tile : 8 * tile + 8, 63:64], (8, 128))

    @pl.when(row == 0)
    def _():
        planes[0, 0, :, :] = jnp.zeros((48, 128), F32)

    @pl.when(row == ROWS - 1)
    def _():
        planes[0, 65, :, :] = jnp.zeros((48, 128), F32)

    for copy in sides:
        copy.wait()
    unpack_sides(0, x)
    side_edges(x)
    for copy in rows:
        copy.wait()
    unpack_rows(0, x)
    other_edges(x, z)

    pack(z)
    rows = row_copies(1, z, 2, 12)
    sides = side_copies(1, 14)
    for copy in rows + sides:
        copy.start()
    acc[...] = jnp.zeros_like(acc)

    @pl.loop(0, 2)
    def _(h):
        acc[...] += gram_of(chunk(z, h))

    g[...] = close_gram(acc[...]).reshape(8, 16, 128)
    reduce = Reduce(row, col, g, inner, part, outer, total, sems)
    reduce.scatter()
    inside(z, x)
    reduce.exchange()
    for copy in sides:
        copy.wait()
    unpack_sides(1, z)
    side_edges(z)
    for copy in rows:
        copy.wait()
    unpack_rows(1, z)
    reduce.gather()
    other_edges(z, x)
    gram = reduce.finish()

    inverse, logs = factor([gram[8 * i : 8 * i + 8, :] for i in range(16)])
    logs_ref[...] = logs
    weights = weights_of(inverse)
    acc[...] = jnp.zeros_like(acc)

    @pl.loop(0, 2)
    def _(h):
        normal = apply_inverse(chunk(x, h), weights)
        for q in range(3):
            b[q, pl.ds(32 * h, 32), :, :] = normal[1024 * q : 1024 * q + 1024, :].reshape(32, LON, MODES)
        acc[...] += gram_of(normal)

    g2[...] = close_gram(acc[...]).reshape(8, 16, 128)
    second = Reduce(row, col, g2, inner2, part2, outer2, total2, sems2)
    second.scatter()
    second.exchange()
    second.gather()
    gram_ref[...] = second.finish()


def start(tangents, fields):
    return pl.pallas_call(
        start_kernel,
        out_shape=(
            jax.ShapeDtypeStruct(tangents.shape, F32),
            jax.ShapeDtypeStruct((MODES, MODES), F32),
            jax.ShapeDtypeStruct((1, MODES), F32),
        ),
        in_specs=[HBM, VMEM],
        out_specs=(VMEM, VMEM, VMEM),
        scratch_shapes=[
            vmem(3, 68, 48, 128), vmem(3, 66, 48, 128), vmem(3, 68, 48, 128), vmem(3, 66, 48, 128), vmem(3, 48, 128), vmem(3, 32, 128),
            vmem(3, 32, 128), vmem(72, 128), vmem(128, 256),
            vmem(3, 16, 8, 128), vmem(3, 16, 8, 128), vmem(2, 3, 16, 8, 128), vmem(2, 3, 16, 8, 128), vmem(4, 8, 128), vmem(2, 4, 8, 128),
            vmem(2, 2, 3, 2, LON, 128),
            *REDUCE_SCRATCH, pltpu.SemaphoreType.DMA((6,)),
            *REDUCE_SCRATCH, pltpu.SemaphoreType.DMA((6,)),
            pltpu.SemaphoreType.DMA((40,)), pltpu.SemaphoreType.DMA((1,)),
        ],
        compiler_params=pltpu.CompilerParams(collective_id=0, has_side_effects=True, vmem_limit_bytes=48 * 2**20),
        name="start",
    )(tangents, fields)


def finish_kernel(b_ref, gram_ref, logs_ref, out_hbm, growth_ref, out, sems):
    inverse, logs = factor([gram_ref[8 * i : 8 * i + 8, :] for i in range(16)])
    weights = weights_of(inverse)
    growth_ref[...] = logs_ref[...] + logs
    rows = out.shape[0] // 4
    copies = []
    for k in range(4):
        here = pl.ds(rows * k, rows)
        out[here, :] = apply_inverse(b_ref[here, :], weights)
        copies.append(pltpu.make_async_copy(out.at[here], out_hbm.at[here], sems.at[k]))
        copies[-1].start()
    for copy in copies:
        copy.wait()


def finish(state, gram, logs):
    return pl.pallas_call(
        finish_kernel,
        out_shape=(jax.ShapeDtypeStruct(state.shape, F32), jax.ShapeDtypeStruct((1, MODES), F32)),
        in_specs=[VMEM, VMEM, VMEM],
        out_specs=(HBM, VMEM),
        scratch_shapes=[vmem(*state.shape), pltpu.SemaphoreType.DMA((4,))],
        compiler_params=pltpu.CompilerParams(vmem_limit_bytes=16 * 2**20),
        name="finish",
    )(state, gram, logs)


def body(tangents, sea_mask, levels, current):
    depth = (levels.T + 1).astype(F32) / LEVELS
    fields = jnp.stack([sea_mask.T.astype(F32), 0.5 * current.T, 0.5 * depth])
    state, gram, logs = start(tangents, fields)
    out, growth = finish(state.reshape(-1, MODES), gram, logs)
    return out.reshape(tangents.shape), growth[0]


def solution(mesh):
    placed = (P(None, "row", "col", None), P("row", "col"), P("row", "col"), P("row", "col"))
    return jax.shard_map(
        body,
        mesh=mesh,
        in_specs=placed,
        out_specs=(P(None, "row", "col", None), P()),
        check_vma=False,
    )
```

```python
import jax
import jax.numpy as jnp
from jax import lax
from jax.experimental import pallas as pl
from jax.experimental.pallas import tpu as pltpu
from jax.sharding import PartitionSpec as P

MESH = pl.DeviceIdType.MESH
F32 = jnp.float32
BF16 = jnp.bfloat16
ROWS, COLS = 8, 16
LAT, LON, MODES = 64, 32, 128
LEVELS = 50
CELLS = 512 * 512
ANY = pl.BlockSpec(memory_space=pl.ANY)
VMEM = pl.BlockSpec(memory_space=pltpu.VMEM)
HBM = pl.BlockSpec(memory_space=pltpu.HBM)


def vmem(*shape):
    return pltpu.VMEM(shape, F32)


def remote(src, dst, sems, k, dev):
    return pltpu.make_async_remote_copy(
        src_ref=src, dst_ref=dst, send_sem=sems.at[2 * k], recv_sem=sems.at[2 * k + 1], device_id=dev, device_id_type=MESH
    )


def at(row, col):
    return {"row": row, "col": col}


def shift(row, col, drow, dcol):
    return at(lax.rem(row + drow + ROWS, ROWS), lax.rem(col + dcol + COLS, COLS))


def inner_peer(row, col, d):
    member = lax.rem(lax.rem(col, 8) + d, 8)
    return member, at(row, (col // 8) * 8 + member)


def outer_index(row, col):
    return (col // 8) * 8 + row


OUTER = [(1, 0, 2), (1, 0, 1), (1, 0, 3), (0, 1, 2), (1, 1, 2), (0, 0, 2), (1, 0, 0), (0, 1, 1), (0, 1, 3), (1, 1, 1), (1, 1, 3)]
OUTER += [(0, 0, 1), (0, 0, 3), (0, 1, 0), (1, 1, 0)]
INNER = (4, 5, 3, 6, 2, 7, 1)


def outer_peer(row, col, step):
    high, low, dz = step
    x_high, z = lax.rem(row // 4 + high, 2), lax.rem(lax.rem(row, 4) + dz, 4)
    return at(4 * x_high + z, 8 * lax.rem(col // 8 + low, 2) + lax.rem(col, 8))


NEIGHBOURS = [(0, -1), (0, 1), (-1, 0), (1, 0), (-1, -1), (-1, 1), (1, -1), (1, 1)]


def greet(row, col):
    barrier = pltpu.get_barrier_semaphore()
    peers = [shift(row, col, a, b) for a, b in NEIGHBOURS[::-1]]
    peers += [outer_peer(row, col, step) for step in OUTER] + [inner_peer(row, col, d)[1] for d in INNER]
    for dev in peers:
        pl.semaphore_signal(barrier, inc=1, device_id=dev, device_id_type=MESH)
    return lambda: pl.semaphore_wait(barrier, len(peers))


class Reduce:
    def __init__(self, row, col, g, inner, part, outer, total, sems):
        self.row, self.col = row, col
        self.g, self.inner, self.part, self.outer, self.total, self.sems = g, inner, part, outer, total, sems
        self.me = lax.rem(col, 8)
        self.waits = []

    def scatter(self):
        for d in INNER:
            member, dev = inner_peer(self.row, self.col, d)
            remote(self.g.at[member], self.inner.at[d], self.sems, 0, dev).start()

    def exchange(self):
        w = remote(self.inner.at[pl.ds(1, 7)], self.inner.at[pl.ds(1, 7)], self.sems, 0, inner_peer(self.row, self.col, 1)[1])
        w.wait_recv()
        s = self.g[self.me]
        for d in range(1, 8):
            s = s + self.inner[d]
        self.part[...] = s
        k = outer_index(self.row, self.col)
        for step in OUTER:
            remote(self.part, self.outer.at[k], self.sems, 1, outer_peer(self.row, self.col, step)).start()
        self.outer[k] = s
        self.waits.append(w)

    def gather(self):
        w = remote(self.outer.at[pl.ds(0, 15)], self.outer.at[pl.ds(0, 15)], self.sems, 1, outer_peer(self.row, self.col, OUTER[0]))
        w.wait_recv()
        t = self.outer[0]
        for e in range(1, 16):
            t = t + self.outer[e]
        self.total[self.me] = t
        for d in INNER:
            remote(self.total.at[self.me], self.total.at[self.me], self.sems, 2, inner_peer(self.row, self.col, d)[1]).start()
        self.waits.append(w)

    def finish(self):
        w = remote(self.total.at[pl.ds(0, 7)], self.total.at[pl.ds(0, 7)], self.sems, 2, inner_peer(self.row, self.col, 1)[1])
        w.wait_recv()
        self.waits.append(w)
        for w in self.waits:
            w.wait_send()
        return self.total[...].reshape(MODES, MODES)


REDUCE_SCRATCH = [vmem(8, 16, 128), vmem(8, 16, 128), vmem(16, 128), vmem(16, 16, 128), vmem(8, 16, 128)]


def split(x):
    hi = x.astype(BF16)
    return hi, (x - hi.astype(F32)).astype(BF16)


def gram_of(x):
    hi, lo = split(x)
    return lax.dot_general(hi, jnp.concatenate([hi, lo], axis=1), (((0,), (0,)), ((), ())), preferred_element_type=F32)


def close_gram(acc):
    cross = acc[:, 128:]
    return (acc[:, :128] + cross + cross.T) * (1.0 / CELLS)


def weights_of(inverse):
    hi, lo = split(inverse)
    return jnp.concatenate(
        [jnp.concatenate([hi, hi], axis=1), jnp.concatenate([lo, jnp.zeros_like(lo)], axis=1)], axis=0
    )


def apply_inverse(x, weights):
    hi, lo = split(x)
    both = lax.dot_general(
        jnp.concatenate([hi, lo], axis=1), weights, (((1,), (1,)), ((), ())), preferred_element_type=F32
    )
    return both[:, :128] + both[:, 128:]


def lanes(x, k):
    return jnp.broadcast_to(x[:, k : k + 1], (8, 128))


def sublanes(x, s):
    return jnp.broadcast_to(x[s : s + 1, :], (8, 128))


def factor(blocks):
    sub = lax.broadcasted_iota(jnp.int32, (8, 128), 0)
    lane = lax.broadcasted_iota(jnp.int32, (8, 128), 1)
    below = [sub > s for s in range(8)]
    w = list(blocks)
    for b in range(16):
        inside = (lane >= 8 * b) & (lane < 8 * b + 8)
        p = w[b]
        c = [lanes(p, 8 * b + m) for m in range(8)]
        upper, scales, pivot_rows = {}, [], []
        for s in range(8):
            here = lane == 8 * b + s
            scale = sublanes(1.0 / c[s], s)
            column = jnp.where(below[s], c[s], 0.0)
            for m in range(s + 1, 8):
                upper[s, m] = sublanes(c[m], s)
            for m in range(s + 1, 8):
                c[m] = c[m] - column * (scale * upper[s, m])
            row = jnp.where(here, 1.0, sublanes(p, s))
            if s < 7:
                p = jnp.where(here & below[s], 0.0, p) - column * (scale * row)
            scales.append(scale)
            pivot_rows.append(jnp.where(inside & (lane > 8 * b + s), 0.0, row))
        w[b] = p
        for j in range(b + 1, 16):
            a = [lanes(w[j], 8 * b + m) for m in range(8)]
            t = jnp.where(inside, 0.0, w[j])
            for s in range(8):
                multiplier = a[s] * scales[s]
                for m in range(s + 1, 8):
                    a[m] = a[m] - multiplier * upper[s, m]
                t = t - multiplier * pivot_rows[s]
            w[j] = t
    diagonal = jnp.zeros((8, 128), F32)
    inverse = []
    for i in range(16):
        on = lane == sub + 8 * i
        pivots = jnp.where(on, w[i], 0.0)
        diagonal = diagonal + pivots
        root = lax.rsqrt(jnp.sum(pivots, axis=1, keepdims=True))
        inverse.append(jnp.where(lane < sub + 8 * i, w[i], jnp.where(on, 1.0, 0.0)) * root)
    return jnp.concatenate(inverse, axis=0), 0.5 * jnp.log(jnp.sum(diagonal, axis=0, keepdims=True))


def model_step(src, src_row, dst, dst_row, planes, spin, count, lat_of, starts):
    @pl.loop(0, count)
    def _(i):
        lat = lat_of(i)
        r, p, o = src_row + lat, 1 + lat, dst_row + lat
        cor = jnp.broadcast_to(spin[pl.ds(p, 1), :], (8, 128))
        for s in starts:
            here = pl.ds(s, 8)
            sea, flow, deep = planes[0, p, here, :], planes[1, p, here, :], planes[2, p, here, :]
            mid = [src[q, r, here, :] for q in range(3)]
            east = [src[q, r, pl.ds(s + 1, 8), :] for q in range(3)]
            west = [src[q, r, pl.ds(s - 1, 8), :] for q in range(3)]
            north = [src[q, r + 1, here, :] for q in range(3)]
            south = [src[q, r - 1, here, :] for q in range(3)]
            along = [east[q] - west[q] for q in range(3)]
            moved = [
                0.4 * mid[q] + 0.15 * ((east[q] + west[q]) + (north[q] + south[q])) - flow * along[q] for q in range(3)
            ]
            dst[0, o, here, :] = sea * (moved[0] - 0.25 * along[2] + cor * mid[1])
            dst[1, o, here, :] = sea * (moved[1] - 0.25 * (north[2] - south[2]) - cor * mid[0])
            dst[2, o, here, :] = sea * (moved[2] - deep * (along[0] + (north[1] - south[1])))


OUTER_STARTS = (7, 15, 23, 31, 39)
INNER_STARTS = (8, 16, 24, 32)


def start_kernel(
    x_hbm, mask_hbm, levels_hbm, current_hbm, b, gram_ref, logs_ref,
    mask_in, levels_in, current_in, x, y, z, planes, table, north_table, south_table, spin, acc,
    send_w, send_e, recv_w, recv_e, send_k, recv_k, ghost,
    g, inner, part, outer, total, sems, g2, inner2, part2, outer2, total2, sems2, hsems, lsem,
):
    row, col = lax.axis_index("row"), lax.axis_index("col")
    load = pltpu.make_async_copy(x_hbm, x.at[:, pl.ds(2, LAT), pl.ds(8, LON), :], lsem.at[0])
    fields = [
        pltpu.make_async_copy(src, dst, lsem.at[k])
        for k, (src, dst) in enumerate(((mask_hbm, mask_in), (levels_hbm, levels_in), (current_hbm, current_in)), 1)
    ]
    for copy in fields:
        copy.start()
    load.start()
    wait_barrier = greet(row, col)

    for copy in fields:
        copy.wait()
    table[0, 8:40, 0:LAT] = mask_in[...].astype(F32)
    table[1, 8:40, 0:LAT] = 0.5 * current_in[...]
    table[2, 8:40, 0:LAT] = 0.5 * ((levels_in[...] + 1).astype(F32) / LEVELS)
    lat = lax.broadcasted_iota(jnp.int32, (72, 128), 0) + row * LAT - 1
    angle = (-70.0 + 140.0 * (lat.astype(F32) + 0.5) / (ROWS * LAT)) * (jnp.pi / 180.0)
    spin[...] = 0.4 * jnp.sin(angle)

    def row_copies(e, src, off, k):
        width = slice(None) if off == 0 else pl.ds(8, LON)
        return [
            remote(src.at[:, pl.ds(off, 2), width, :], ghost.at[e, 1], hsems, k, shift(row, col, -1, 0)),
            remote(src.at[:, pl.ds(off + 62, 2), width, :], ghost.at[e, 0], hsems, k + 1, shift(row, col, 1, 0)),
        ]

    def pack(x):
        @pl.loop(0, 16)
        def _(j):
            for q in range(3):
                for m in range(4):
                    send_w[q, j, 2 * m : 2 * m + 2, :] = x[q, 4 * j + m + 2, 8:10, :]
                    send_e[q, j, 2 * m : 2 * m + 2, :] = x[q, 4 * j + m + 2, 38:40, :]

        for c, (i, j) in enumerate(((2, 8), (2, 39), (65, 8), (65, 39))):
            for q in range(3):
                send_k[c, q : q + 1, :] = x[q, i, j : j + 1, :]

    def side_copies(e, k):
        out = [
            remote(send_w, recv_e.at[e], hsems, k, shift(row, col, 0, -1)),
            remote(send_e, recv_w.at[e], hsems, k + 1, shift(row, col, 0, 1)),
        ]
        for c, (a, b) in enumerate(((-1, -1), (-1, 1), (1, -1), (1, 1))):
            out.append(remote(send_k.at[c], recv_k.at[e, 3 - c], hsems, k + 2 + c, shift(row, col, a, b)))
        return out

    def unpack_sides(e, x):
        @pl.loop(0, 16)
        def _(j):
            for q in range(3):
                for m in range(4):
                    x[q, 4 * j + m + 2, 6:8, :] = recv_w[e, q, j, 2 * m : 2 * m + 2, :]
                    x[q, 4 * j + m + 2, 40:42, :] = recv_e[e, q, j, 2 * m : 2 * m + 2, :]

    def unpack_rows(e, x):
        for c, (i, j) in enumerate(((1, 7), (1, 40), (66, 7), (66, 40))):
            for q in range(3):
                x[q, i, j : j + 1, :] = recv_k[e, c, q : q + 1, :]

        x[:, 0:2, 8:40, :] = ghost[e, 0]
        x[:, 66:68, 8:40, :] = ghost[e, 1]

        @pl.when(row == 0)
        def _():
            x[:, 0:2, :, :] = jnp.zeros((3, 2, 48, 128), F32)

        @pl.when(row == ROWS - 1)
        def _():
            x[:, 66:68, :, :] = jnp.zeros((3, 2, 48, 128), F32)

    def spread(k, tile):
        start = pl.multiple_of(8 * tile, 8)
        lanes = table[k, pl.ds(start, 8), :]
        for i in range(LAT):
            planes[k, i + 1, pl.ds(start, 8), :] = jnp.broadcast_to(lanes[:, i : i + 1], (8, 128))

    def chunk(x, h):
        return jnp.concatenate([x[q, pl.ds(32 * h + 2, 32), 8:40, :].reshape(1024, MODES) for q in range(3)], axis=0)

    def inside(x, z):
        model_step(x, 2, y, 1, planes, spin, LAT - 2, lambda i: i + 1, INNER_STARTS)
        model_step(y, 1, z, 2, planes, spin, LAT - 4, lambda i: i + 2, INNER_STARTS)

    def side_edges(x):
        model_step(x, 2, y, 1, planes, spin, LAT - 2, lambda i: i + 1, (7, 33))

    def other_edges(x, z):
        model_step(x, 2, y, 1, planes, spin, 4, lambda i: i - 1 + 62 * (i // 2), OUTER_STARTS)
        model_step(y, 1, z, 2, planes, spin, 4, lambda i: i + 60 * (i // 2), INNER_STARTS)
        model_step(y, 1, z, 2, planes, spin, LAT - 4, lambda i: i + 2, (8, 32))

    rows = row_copies(0, x_hbm, 0, 0)
    sides = side_copies(0, 2)
    tables = [
        remote(table.at[:, pl.ds(8, 8), :], table.at[:, pl.ds(40, 8), :], hsems, 8, shift(row, col, 0, -1)),
        remote(table.at[:, pl.ds(32, 8), :], table.at[:, pl.ds(0, 8), :], hsems, 9, shift(row, col, 0, 1)),
        remote(table.at[:, pl.ds(8, 32), :], north_table, hsems, 10, shift(row, col, -1, 0)),
        remote(table.at[:, pl.ds(8, 32), :], south_table, hsems, 11, shift(row, col, 1, 0)),
    ]
    for k in range(3):
        @pl.loop(1, 5)
        def _(tile):
            spread(k, tile)

    load.wait()
    pack(x)
    wait_barrier()
    for copy in sides[2:] + tables + sides[:2] + rows:
        copy.start()
    inside(x, z)
    for copy in tables:
        copy.wait()
    for k in range(3):
        @pl.loop(0, 2)
        def _(edge):
            spread(k, 5 * edge)

        for tile in range(4):
            planes[k, 65, 8 * tile + 8 : 8 * tile + 16, :] = jnp.broadcast_to(north_table[k, 8 * tile : 8 * tile + 8, 0:1], (8, 128))
            planes[k, 0, 8 * tile + 8 : 8 * tile + 16, :] = jnp.broadcast_to(south_table[k, 8 * tile : 8 * tile + 8, 63:64], (8, 128))

    @pl.when(row == 0)
    def _():
        planes[0, 0, :, :] = jnp.zeros((48, 128), F32)

    @pl.when(row == ROWS - 1)
    def _():
        planes[0, 65, :, :] = jnp.zeros((48, 128), F32)

    for copy in sides:
        copy.wait()
    unpack_sides(0, x)
    side_edges(x)
    for copy in rows:
        copy.wait()
    unpack_rows(0, x)
    other_edges(x, z)

    pack(z)
    rows = row_copies(1, z, 2, 12)
    sides = side_copies(1, 14)
    for copy in sides[2:] + rows:
        copy.start()
    acc[...] = jnp.zeros_like(acc)

    @pl.loop(0, 2)
    def _(h):
        acc[...] += gram_of(chunk(z, h))

    g[...] = close_gram(acc[...]).reshape(8, 16, 128)
    reduce = Reduce(row, col, g, inner, part, outer, total, sems)
    reduce.scatter()
    for copy in sides[:2]:
        copy.start()
    inside(z, x)
    reduce.exchange()
    for copy in rows:
        copy.wait()
    reduce.gather()
    for copy in sides:
        copy.wait()
    unpack_sides(1, z)
    side_edges(z)
    unpack_rows(1, z)
    other_edges(z, x)
    gram = reduce.finish()

    inverse, logs = factor([gram[8 * i : 8 * i + 8, :] for i in range(16)])
    logs_ref[...] = logs
    weights = weights_of(inverse)
    acc[...] = jnp.zeros_like(acc)

    @pl.loop(0, 2)
    def _(h):
        normal = apply_inverse(chunk(x, h), weights)
        for q in range(3):
            b[q, pl.ds(32 * h, 32), :, :] = normal[1024 * q : 1024 * q + 1024, :].reshape(32, LON, MODES)
        acc[...] += gram_of(normal)

    g2[...] = close_gram(acc[...]).reshape(8, 16, 128)
    second = Reduce(row, col, g2, inner2, part2, outer2, total2, sems2)
    second.scatter()
    second.exchange()
    second.gather()
    gram_ref[...] = second.finish()


def start(tangents, *fields):
    return pl.pallas_call(
        start_kernel,
        out_shape=(
            jax.ShapeDtypeStruct(tangents.shape, F32),
            jax.ShapeDtypeStruct((MODES, MODES), F32),
            jax.ShapeDtypeStruct((1, MODES), F32),
        ),
        in_specs=[HBM] * 4,
        out_specs=(VMEM, VMEM, VMEM),
        scratch_shapes=[
            pltpu.VMEM((LON, LAT), jnp.int32), pltpu.VMEM((LON, LAT), jnp.int32), vmem(LON, LAT),
            vmem(3, 68, 48, 128), vmem(3, 66, 48, 128), vmem(3, 68, 48, 128), vmem(3, 66, 48, 128), vmem(3, 48, 128), vmem(3, 32, 128),
            vmem(3, 32, 128), vmem(72, 128), vmem(128, 256),
            vmem(3, 16, 8, 128), vmem(3, 16, 8, 128), vmem(2, 3, 16, 8, 128), vmem(2, 3, 16, 8, 128), vmem(4, 8, 128), vmem(2, 4, 8, 128),
            vmem(2, 2, 3, 2, LON, 128),
            *REDUCE_SCRATCH, pltpu.SemaphoreType.DMA((6,)),
            *REDUCE_SCRATCH, pltpu.SemaphoreType.DMA((6,)),
            pltpu.SemaphoreType.DMA((40,)), pltpu.SemaphoreType.DMA((4,)),
        ],
        compiler_params=pltpu.CompilerParams(collective_id=0, has_side_effects=True, vmem_limit_bytes=48 * 2**20),
        name="start",
    )(tangents, *fields)


def finish_kernel(b_ref, gram_ref, logs_ref, out_hbm, growth_ref, out, sems):
    inverse, logs = factor([gram_ref[8 * i : 8 * i + 8, :] for i in range(16)])
    weights = weights_of(inverse)
    growth_ref[...] = logs_ref[...] + logs
    rows = out.shape[0] // 4
    copies = []
    for k in range(4):
        here = pl.ds(rows * k, rows)
        out[here, :] = apply_inverse(b_ref[here, :], weights)
        copies.append(pltpu.make_async_copy(out.at[here], out_hbm.at[here], sems.at[k]))
        copies[-1].start()
    for copy in copies:
        copy.wait()


def finish(state, gram, logs):
    return pl.pallas_call(
        finish_kernel,
        out_shape=(jax.ShapeDtypeStruct(state.shape, F32), jax.ShapeDtypeStruct((1, MODES), F32)),
        in_specs=[VMEM, VMEM, VMEM],
        out_specs=(HBM, VMEM),
        scratch_shapes=[vmem(*state.shape), pltpu.SemaphoreType.DMA((4,))],
        compiler_params=pltpu.CompilerParams(vmem_limit_bytes=16 * 2**20),
        name="finish",
    )(state, gram, logs)


def body(tangents, sea_mask, levels, current):
    fields = [pltpu.with_memory_space_constraint(v.T, pltpu.HBM) for v in (sea_mask, levels, current)]
    state, gram, logs = start(tangents, *fields)
    out, growth = finish(state.reshape(-1, MODES), gram, logs)
    return out.reshape(tangents.shape), growth[0]


def solution(mesh):
    placed = (P(None, "row", "col", None), P("row", "col"), P("row", "col"), P("row", "col"))
    return jax.shard_map(
        body,
        mesh=mesh,
        in_specs=placed,
        out_specs=(P(None, "row", "col", None), P()),
        check_vma=False,
    )
```

```python
import jax
import jax.numpy as jnp
from jax import lax
from jax.experimental import pallas as pl
from jax.experimental.pallas import tpu as pltpu
from jax.sharding import PartitionSpec as P

MESH = pl.DeviceIdType.MESH
F32 = jnp.float32
BF16 = jnp.bfloat16
ROWS, COLS = 8, 16
LAT, LON, MODES = 64, 32, 128
LEVELS = 50
CELLS = 512 * 512
ANY = pl.BlockSpec(memory_space=pl.ANY)
VMEM = pl.BlockSpec(memory_space=pltpu.VMEM)
HBM = pl.BlockSpec(memory_space=pltpu.HBM)


def vmem(*shape):
    return pltpu.VMEM(shape, F32)


def remote(src, dst, sems, k, dev):
    return pltpu.make_async_remote_copy(
        src_ref=src, dst_ref=dst, send_sem=sems.at[2 * k], recv_sem=sems.at[2 * k + 1], device_id=dev, device_id_type=MESH
    )


def at(row, col):
    return {"row": row, "col": col}


def shift(row, col, drow, dcol):
    return at(lax.rem(row + drow + ROWS, ROWS), lax.rem(col + dcol + COLS, COLS))


def inner_peer(row, col, d):
    member = lax.rem(lax.rem(col, 8) + d, 8)
    return member, at(row, (col // 8) * 8 + member)


def outer_index(row, col):
    return (col // 8) * 8 + row


OUTER = [(1, 0, 2), (1, 0, 1), (1, 0, 3), (0, 1, 2), (1, 1, 2), (0, 0, 2), (1, 0, 0), (0, 1, 1), (0, 1, 3), (1, 1, 1), (1, 1, 3)]
OUTER += [(0, 0, 1), (0, 0, 3), (0, 1, 0), (1, 1, 0)]
INNER = (4, 5, 3, 6, 2, 7, 1)


def outer_peer(row, col, step):
    high, low, dz = step
    x_high, z = lax.rem(row // 4 + high, 2), lax.rem(lax.rem(row, 4) + dz, 4)
    return at(4 * x_high + z, 8 * lax.rem(col // 8 + low, 2) + lax.rem(col, 8))


NEIGHBOURS = [(0, -1), (0, 1), (-1, 0), (1, 0), (-1, -1), (-1, 1), (1, -1), (1, 1)]


def greet(row, col):
    barrier = pltpu.get_barrier_semaphore()
    peers = [shift(row, col, a, b) for a, b in NEIGHBOURS[::-1]]
    peers += [outer_peer(row, col, step) for step in OUTER] + [inner_peer(row, col, d)[1] for d in INNER]
    for dev in peers:
        pl.semaphore_signal(barrier, inc=1, device_id=dev, device_id_type=MESH)
    return lambda: pl.semaphore_wait(barrier, len(peers))


class Reduce:
    def __init__(self, row, col, g, inner, part, outer, total, sems):
        self.row, self.col = row, col
        self.g, self.inner, self.part, self.outer, self.total, self.sems = g, inner, part, outer, total, sems
        self.me = lax.rem(col, 8)
        self.waits = []

    def scatter(self):
        for d in INNER:
            member, dev = inner_peer(self.row, self.col, d)
            remote(self.g.at[member], self.inner.at[d], self.sems, 0, dev).start()

    def exchange(self):
        w = remote(self.inner.at[pl.ds(1, 7)], self.inner.at[pl.ds(1, 7)], self.sems, 0, inner_peer(self.row, self.col, 1)[1])
        w.wait_recv()
        s = self.g[self.me]
        for d in range(1, 8):
            s = s + self.inner[d]
        self.part[...] = s
        k = outer_index(self.row, self.col)
        for step in OUTER:
            remote(self.part, self.outer.at[k], self.sems, 1, outer_peer(self.row, self.col, step)).start()
        self.outer[k] = s
        self.waits.append(w)

    def gather(self):
        w = remote(self.outer.at[pl.ds(0, 15)], self.outer.at[pl.ds(0, 15)], self.sems, 1, outer_peer(self.row, self.col, OUTER[0]))
        w.wait_recv()
        t = self.outer[0]
        for e in range(1, 16):
            t = t + self.outer[e]
        self.total[self.me] = t
        for d in INNER:
            remote(self.total.at[self.me], self.total.at[self.me], self.sems, 2, inner_peer(self.row, self.col, d)[1]).start()
        self.waits.append(w)

    def finish(self):
        w = remote(self.total.at[pl.ds(0, 7)], self.total.at[pl.ds(0, 7)], self.sems, 2, inner_peer(self.row, self.col, 1)[1])
        w.wait_recv()
        self.waits.append(w)
        for w in self.waits:
            w.wait_send()
        return self.total[...].reshape(MODES, MODES)


REDUCE_SCRATCH = [vmem(8, 16, 128), vmem(8, 16, 128), vmem(16, 128), vmem(16, 16, 128), vmem(8, 16, 128)]


def split(x):
    hi = x.astype(BF16)
    return hi, (x - hi.astype(F32)).astype(BF16)


def gram_of(x):
    hi, lo = split(x)
    return lax.dot_general(hi, jnp.concatenate([hi, lo], axis=1), (((0,), (0,)), ((), ())), preferred_element_type=F32)


def close_gram(acc):
    cross = acc[:, 128:]
    return (acc[:, :128] + cross + cross.T) * (1.0 / CELLS)


def weights_of(inverse):
    hi, lo = split(inverse)
    return jnp.concatenate(
        [jnp.concatenate([hi, hi], axis=1), jnp.concatenate([lo, jnp.zeros_like(lo)], axis=1)], axis=0
    )


def apply_inverse(x, weights):
    hi, lo = split(x)
    both = lax.dot_general(
        jnp.concatenate([hi, lo], axis=1), weights, (((1,), (1,)), ((), ())), preferred_element_type=F32
    )
    return both[:, :128] + both[:, 128:]


def lanes(x, k):
    return jnp.broadcast_to(x[:, k : k + 1], (8, 128))


def sublanes(x, s):
    return jnp.broadcast_to(x[s : s + 1, :], (8, 128))


def factor(blocks):
    sub = lax.broadcasted_iota(jnp.int32, (8, 128), 0)
    lane = lax.broadcasted_iota(jnp.int32, (8, 128), 1)
    below = [sub > s for s in range(8)]
    w = list(blocks)
    for b in range(16):
        inside = (lane >= 8 * b) & (lane < 8 * b + 8)
        p = w[b]
        c = [lanes(p, 8 * b + m) for m in range(8)]
        upper, scales, pivot_rows = {}, [], []
        for s in range(8):
            here = lane == 8 * b + s
            scale = sublanes(1.0 / c[s], s)
            column = jnp.where(below[s], c[s], 0.0)
            for m in range(s + 1, 8):
                upper[s, m] = sublanes(c[m], s)
            for m in range(s + 1, 8):
                c[m] = c[m] - column * (scale * upper[s, m])
            row = jnp.where(here, 1.0, sublanes(p, s))
            if s < 7:
                p = jnp.where(here & below[s], 0.0, p) - column * (scale * row)
            scales.append(scale)
            pivot_rows.append(jnp.where(inside & (lane > 8 * b + s), 0.0, row))
        w[b] = p
        for j in range(b + 1, 16):
            a = [lanes(w[j], 8 * b + m) for m in range(8)]
            t = jnp.where(inside, 0.0, w[j])
            for s in range(8):
                multiplier = a[s] * scales[s]
                for m in range(s + 1, 8):
                    a[m] = a[m] - multiplier * upper[s, m]
                t = t - multiplier * pivot_rows[s]
            w[j] = t
    diagonal = jnp.zeros((8, 128), F32)
    inverse = []
    for i in range(16):
        on = lane == sub + 8 * i
        pivots = jnp.where(on, w[i], 0.0)
        diagonal = diagonal + pivots
        root = lax.rsqrt(jnp.sum(pivots, axis=1, keepdims=True))
        inverse.append(jnp.where(lane < sub + 8 * i, w[i], jnp.where(on, 1.0, 0.0)) * root)
    return jnp.concatenate(inverse, axis=0), 0.5 * jnp.log(jnp.sum(diagonal, axis=0, keepdims=True))


def model_step(src, src_row, dst, dst_row, planes, spin, count, lat_of, starts):
    @pl.loop(0, count)
    def _(i):
        lat = lat_of(i)
        r, p, o = src_row + lat, 1 + lat, dst_row + lat
        cor = jnp.broadcast_to(spin[pl.ds(p, 1), :], (8, 128))
        for s in starts:
            here = pl.ds(s, 8)
            sea, flow, deep = planes[0, p, here, :], planes[1, p, here, :], planes[2, p, here, :]
            mid = [src[q, r, here, :] for q in range(3)]
            east = [src[q, r, pl.ds(s + 1, 8), :] for q in range(3)]
            west = [src[q, r, pl.ds(s - 1, 8), :] for q in range(3)]
            north = [src[q, r + 1, here, :] for q in range(3)]
            south = [src[q, r - 1, here, :] for q in range(3)]
            along = [east[q] - west[q] for q in range(3)]
            moved = [
                0.4 * mid[q] + 0.15 * ((east[q] + west[q]) + (north[q] + south[q])) - flow * along[q] for q in range(3)
            ]
            dst[0, o, here, :] = sea * (moved[0] - 0.25 * along[2] + cor * mid[1])
            dst[1, o, here, :] = sea * (moved[1] - 0.25 * (north[2] - south[2]) - cor * mid[0])
            dst[2, o, here, :] = sea * (moved[2] - deep * (along[0] + (north[1] - south[1])))


OUTER_STARTS = (7, 15, 23, 31, 39)
INNER_STARTS = (8, 16, 24, 32)


def start_kernel(
    x_hbm, mask_hbm, levels_hbm, current_hbm, b, gram_ref, logs_ref,
    mask_in, levels_in, current_in, x, y, z, planes, table, north_table, south_table, spin, acc,
    send_w, send_e, recv_w, recv_e, send_k, recv_k, ghost,
    g, inner, part, outer, total, sems, g2, inner2, part2, outer2, total2, sems2, hsems, lsem,
):
    row, col = lax.axis_index("row"), lax.axis_index("col")
    load = pltpu.make_async_copy(x_hbm, x.at[:, pl.ds(2, LAT), pl.ds(8, LON), :], lsem.at[0])
    fields = [
        pltpu.make_async_copy(src, dst, lsem.at[k])
        for k, (src, dst) in enumerate(((mask_hbm, mask_in), (levels_hbm, levels_in), (current_hbm, current_in)), 1)
    ]
    for copy in fields:
        copy.start()
    load.start()
    wait_barrier = greet(row, col)

    for copy in fields:
        copy.wait()
    table[0, 8:40, 0:LAT] = mask_in[...].astype(F32)
    table[1, 8:40, 0:LAT] = 0.5 * current_in[...]
    table[2, 8:40, 0:LAT] = 0.5 * ((levels_in[...] + 1).astype(F32) / LEVELS)
    lat = lax.broadcasted_iota(jnp.int32, (72, 128), 0) + row * LAT - 1
    angle = (-70.0 + 140.0 * (lat.astype(F32) + 0.5) / (ROWS * LAT)) * (jnp.pi / 180.0)
    spin[...] = 0.4 * jnp.sin(angle)

    def row_copies(e, src, off, k):
        width = slice(None) if off == 0 else pl.ds(8, LON)
        return [
            remote(src.at[:, pl.ds(off, 2), width, :], ghost.at[e, 1], hsems, k, shift(row, col, -1, 0)),
            remote(src.at[:, pl.ds(off + 62, 2), width, :], ghost.at[e, 0], hsems, k + 1, shift(row, col, 1, 0)),
        ]

    def pack(x):
        @pl.loop(0, 16)
        def _(j):
            for q in range(3):
                for m in range(4):
                    send_w[q, j, 2 * m : 2 * m + 2, :] = x[q, 4 * j + m + 2, 8:10, :]
                    send_e[q, j, 2 * m : 2 * m + 2, :] = x[q, 4 * j + m + 2, 38:40, :]

        for c, (i, j) in enumerate(((2, 8), (2, 39), (65, 8), (65, 39))):
            for q in range(3):
                send_k[c, q : q + 1, :] = x[q, i, j : j + 1, :]

    def side_copies(e, k):
        out = [
            remote(send_w, recv_e.at[e], hsems, k, shift(row, col, 0, -1)),
            remote(send_e, recv_w.at[e], hsems, k + 1, shift(row, col, 0, 1)),
        ]
        for c, (a, b) in enumerate(((-1, -1), (-1, 1), (1, -1), (1, 1))):
            out.append(remote(send_k.at[c], recv_k.at[e, 3 - c], hsems, k + 2 + c, shift(row, col, a, b)))
        return out

    def unpack_sides(e, x):
        @pl.loop(0, 16)
        def _(j):
            for q in range(3):
                for m in range(4):
                    x[q, 4 * j + m + 2, 6:8, :] = recv_w[e, q, j, 2 * m : 2 * m + 2, :]
                    x[q, 4 * j + m + 2, 40:42, :] = recv_e[e, q, j, 2 * m : 2 * m + 2, :]

    def unpack_rows(e, x):
        for c, (i, j) in enumerate(((1, 7), (1, 40), (66, 7), (66, 40))):
            for q in range(3):
                x[q, i, j : j + 1, :] = recv_k[e, c, q : q + 1, :]

        x[:, 0:2, 8:40, :] = ghost[e, 0]
        x[:, 66:68, 8:40, :] = ghost[e, 1]

        @pl.when(row == 0)
        def _():
            x[:, 0:2, :, :] = jnp.zeros((3, 2, 48, 128), F32)

        @pl.when(row == ROWS - 1)
        def _():
            x[:, 66:68, :, :] = jnp.zeros((3, 2, 48, 128), F32)

    def spread(k, tile):
        start = pl.multiple_of(8 * tile, 8)
        lanes = table[k, pl.ds(start, 8), :]
        for i in range(LAT):
            planes[k, i + 1, pl.ds(start, 8), :] = jnp.broadcast_to(lanes[:, i : i + 1], (8, 128))

    def chunk(x, h):
        return jnp.concatenate([x[q, pl.ds(32 * h + 2, 32), 8:40, :].reshape(1024, MODES) for q in range(3)], axis=0)

    def inside(x, z):
        model_step(x, 2, y, 1, planes, spin, LAT - 2, lambda i: i + 1, INNER_STARTS)
        model_step(y, 1, z, 2, planes, spin, LAT - 4, lambda i: i + 2, INNER_STARTS)

    def side_edges(x):
        model_step(x, 2, y, 1, planes, spin, LAT - 2, lambda i: i + 1, (7, 33))

    def other_edges(x, z):
        model_step(x, 2, y, 1, planes, spin, 4, lambda i: i - 1 + 62 * (i // 2), OUTER_STARTS)
        model_step(y, 1, z, 2, planes, spin, 4, lambda i: i + 60 * (i // 2), INNER_STARTS)
        model_step(y, 1, z, 2, planes, spin, LAT - 4, lambda i: i + 2, (8, 32))

    rows = row_copies(0, x_hbm, 0, 0)
    sides = side_copies(0, 2)
    tables = [
        remote(table.at[:, pl.ds(8, 8), :], table.at[:, pl.ds(40, 8), :], hsems, 8, shift(row, col, 0, -1)),
        remote(table.at[:, pl.ds(32, 8), :], table.at[:, pl.ds(0, 8), :], hsems, 9, shift(row, col, 0, 1)),
        remote(table.at[:, pl.ds(8, 32), :], north_table, hsems, 10, shift(row, col, -1, 0)),
        remote(table.at[:, pl.ds(8, 32), :], south_table, hsems, 11, shift(row, col, 1, 0)),
    ]
    for k in range(3):
        @pl.loop(1, 5)
        def _(tile):
            spread(k, tile)

    load.wait()
    pack(x)
    wait_barrier()
    for copy in sides[2:] + tables + sides[:2] + rows:
        copy.start()
    inside(x, z)
    middle = [z[q, 4:64, 16:32, :].reshape(960, MODES) for q in range(3)]
    acc[...] = gram_of(jnp.concatenate(middle, axis=0))
    for copy in tables:
        copy.wait()
    for k in range(3):
        @pl.loop(0, 2)
        def _(edge):
            spread(k, 5 * edge)

        for tile in range(4):
            planes[k, 65, 8 * tile + 8 : 8 * tile + 16, :] = jnp.broadcast_to(north_table[k, 8 * tile : 8 * tile + 8, 0:1], (8, 128))
            planes[k, 0, 8 * tile + 8 : 8 * tile + 16, :] = jnp.broadcast_to(south_table[k, 8 * tile : 8 * tile + 8, 63:64], (8, 128))

    @pl.when(row == 0)
    def _():
        planes[0, 0, :, :] = jnp.zeros((48, 128), F32)

    @pl.when(row == ROWS - 1)
    def _():
        planes[0, 65, :, :] = jnp.zeros((48, 128), F32)

    for copy in sides:
        copy.wait()
    unpack_sides(0, x)
    side_edges(x)
    for copy in rows:
        copy.wait()
    unpack_rows(0, x)
    other_edges(x, z)

    pack(z)
    rows = row_copies(1, z, 2, 12)
    sides = side_copies(1, 14)
    frame = [z[q, 2:66, c : c + 8, :].reshape(512, MODES) for q in range(3) for c in (8, 32)]
    frame += [z[q, r : r + 2, 16:32, :].reshape(32, MODES) for q in range(3) for r in (2, 64)]
    acc[...] += gram_of(jnp.concatenate(frame, axis=0))
    g[...] = close_gram(acc[...]).reshape(8, 16, 128)
    reduce = Reduce(row, col, g, inner, part, outer, total, sems)
    reduce.scatter()
    for copy in sides[2:] + rows + sides[:2]:
        copy.start()
    inside(z, x)
    reduce.exchange()
    for copy in rows:
        copy.wait()
    reduce.gather()
    for copy in sides:
        copy.wait()
    unpack_sides(1, z)
    side_edges(z)
    unpack_rows(1, z)
    other_edges(z, x)
    gram = reduce.finish()

    inverse, logs = factor([gram[8 * i : 8 * i + 8, :] for i in range(16)])
    logs_ref[...] = logs
    weights = weights_of(inverse)
    acc[...] = jnp.zeros_like(acc)

    @pl.loop(0, 2)
    def _(h):
        normal = apply_inverse(chunk(x, h), weights)
        for q in range(3):
            b[q, pl.ds(32 * h, 32), :, :] = normal[1024 * q : 1024 * q + 1024, :].reshape(32, LON, MODES)
        acc[...] += gram_of(normal)

    g2[...] = close_gram(acc[...]).reshape(8, 16, 128)
    second = Reduce(row, col, g2, inner2, part2, outer2, total2, sems2)
    second.scatter()
    second.exchange()
    second.gather()
    gram_ref[...] = second.finish()


def start(tangents, *fields):
    return pl.pallas_call(
        start_kernel,
        out_shape=(
            jax.ShapeDtypeStruct(tangents.shape, F32),
            jax.ShapeDtypeStruct((MODES, MODES), F32),
            jax.ShapeDtypeStruct((1, MODES), F32),
        ),
        in_specs=[HBM] * 4,
        out_specs=(VMEM, VMEM, VMEM),
        scratch_shapes=[
            pltpu.VMEM((LON, LAT), jnp.int32), pltpu.VMEM((LON, LAT), jnp.int32), vmem(LON, LAT),
            vmem(3, 68, 48, 128), vmem(3, 66, 48, 128), vmem(3, 68, 48, 128), vmem(3, 66, 48, 128), vmem(3, 48, 128), vmem(3, 32, 128),
            vmem(3, 32, 128), vmem(72, 128), vmem(128, 256),
            vmem(3, 16, 8, 128), vmem(3, 16, 8, 128), vmem(2, 3, 16, 8, 128), vmem(2, 3, 16, 8, 128), vmem(4, 8, 128), vmem(2, 4, 8, 128),
            vmem(2, 2, 3, 2, LON, 128),
            *REDUCE_SCRATCH, pltpu.SemaphoreType.DMA((6,)),
            *REDUCE_SCRATCH, pltpu.SemaphoreType.DMA((6,)),
            pltpu.SemaphoreType.DMA((40,)), pltpu.SemaphoreType.DMA((4,)),
        ],
        compiler_params=pltpu.CompilerParams(collective_id=0, has_side_effects=True, vmem_limit_bytes=48 * 2**20),
        name="start",
    )(tangents, *fields)


def finish_kernel(b_ref, gram_ref, logs_ref, out_hbm, growth_ref, out, sems):
    inverse, logs = factor([gram_ref[8 * i : 8 * i + 8, :] for i in range(16)])
    weights = weights_of(inverse)
    growth_ref[...] = logs_ref[...] + logs
    rows = out.shape[0] // 4
    copies = []
    for k in range(4):
        here = pl.ds(rows * k, rows)
        out[here, :] = apply_inverse(b_ref[here, :], weights)
        copies.append(pltpu.make_async_copy(out.at[here], out_hbm.at[here], sems.at[k]))
        copies[-1].start()
    for copy in copies:
        copy.wait()


def finish(state, gram, logs):
    return pl.pallas_call(
        finish_kernel,
        out_shape=(jax.ShapeDtypeStruct(state.shape, F32), jax.ShapeDtypeStruct((1, MODES), F32)),
        in_specs=[VMEM, VMEM, VMEM],
        out_specs=(HBM, VMEM),
        scratch_shapes=[vmem(*state.shape), pltpu.SemaphoreType.DMA((4,))],
        compiler_params=pltpu.CompilerParams(vmem_limit_bytes=16 * 2**20),
        name="finish",
    )(state, gram, logs)


def body(tangents, sea_mask, levels, current):
    fields = [pltpu.with_memory_space_constraint(v.T, pltpu.HBM) for v in (sea_mask, levels, current)]
    state, gram, logs = start(tangents, *fields)
    out, growth = finish(state.reshape(-1, MODES), gram, logs)
    return out.reshape(tangents.shape), growth[0]


def solution(mesh):
    placed = (P(None, "row", "col", None), P("row", "col"), P("row", "col"), P("row", "col"))
    return jax.shard_map(
        body,
        mesh=mesh,
        in_specs=placed,
        out_specs=(P(None, "row", "col", None), P()),
        check_vma=False,
    )
```
